128 devices in a mesh: row: 8 (over z, core), col: 16 (over y, x).
Axes of the slice: x: 4, y: 4, z: 4, core: 2. Of those that a mesh axis runs over, the one named last changes fastest.
Arguments:
- amp_tiles: float32 [16, 32, 256, 256], P('row', 'col'), may hold values from -6 to 6
- int_tiles: float32 [32, 32, 256, 256], P('col', 'row'), may hold values from -0.125 to 0.125
- resid_init: float32 [16, 32, 256, 256], P('row', 'col'), may hold values from -6 to 6
- triples: int32 [8, 16, 3, 32], P('row', 'col'), may hold values from 0 to 1023, as said below
Outputs:
- resid_out: float32 [16, 32, 256, 256], P('row', 'col')
The draws below stay inside these ranges and needn't reach their ends.
Inputs may be any that keep to these rules, and one draw needn't show every extreme that they name: Each triple names tiles (i, j), (j, k), (i, k) with one i, j, k. The amplitude tile of every triple on device (r, c) is one that device holds. For every device and every column index q, exactly 2 distinct residual tiles held at (r, q) are named by that device's triples, each by exactly one of that device's triples. No triple is listed twice; the order of triples on a device is arbitrary.
All inputs are finite; a program needn't handle non-finite values.
Results may differ from the reference program's by a relative error of at most 0.0001.
Values sent between devices are 32-bit elements; how exact they have to be, the bound alone decides.
No kernel may reach another device: no remote copies, remote signals or barrier semaphores. Data moves between devices by JAX's collectives and lax.ppermute only.
A program may use at most 128 MiB of HBM per device.

```python
import jax
import jax.numpy as jnp
from jax import lax

TILE = 256
LI = 2
LJ = 2
CAP = 2
JPER = 1
KC = 2
MI_T = 16
MJ_T = 32
MK = 32
TRIP_DEV = 32
N_ROW = 8
N_COL = 16


def front_perm(key, count, target, active):
    order = jax.random.permutation(key, count).astype(jnp.int32)
    where_at = jnp.argmax((order == target).astype(jnp.int32)).astype(jnp.int32)
    shifted = jnp.roll(order, -where_at)
    return jnp.where(active, shifted, order)


def draw_triples(key, part):
    execs = N_ROW * N_COL
    per_owner = LI * KC
    key_tiles = jax.random.fold_in(key, 101)
    key_vir = jax.random.fold_in(key, 202)
    key_order = jax.random.fold_in(key, 303)
    tile_count = execs * N_COL
    tile_keys = jax.random.split(key_tiles, tile_count)
    tile_flat = jnp.arange(tile_count, dtype=jnp.int32)
    tile_target = jnp.where(tile_flat == 0, 0, per_owner - 1).astype(jnp.int32)
    tile_active = (tile_flat == 0) | (tile_flat == tile_count - 1)
    chosen = jax.vmap(lambda k, t, a: front_perm(k, per_owner, t, a)[:CAP])(tile_keys, tile_target, tile_active)
    chosen = chosen.reshape(execs, N_COL, CAP).astype(jnp.int32)
    vir_count = execs * N_COL * CAP
    vir_keys = jax.random.split(key_vir, vir_count)
    vir_flat = jnp.arange(vir_count, dtype=jnp.int32)
    last_slot = (tile_count - 1) * CAP
    vir_target = jnp.where(vir_flat == 0, 0, LJ - 1).astype(jnp.int32)
    vir_active = (vir_flat == 0) | (vir_flat == last_slot)
    vir_pick = jax.vmap(lambda k, t, a: front_perm(k, LJ, t, a)[:JPER])(vir_keys, vir_target, vir_active)
    vir_pick = vir_pick.reshape(execs, N_COL, CAP, JPER).astype(jnp.int32)
    exec_ids = jnp.arange(execs, dtype=jnp.int32)
    exec_row = (exec_ids // N_COL)[:, None, None, None]
    exec_col = (exec_ids % N_COL)[:, None, None, None]
    owner_col = jnp.arange(N_COL, dtype=jnp.int32)[None, :, None, None]
    tile_local = chosen[:, :, :, None]
    occ_global = exec_row * LI + tile_local // KC
    k_global = owner_col * KC + tile_local % KC
    vir_global = exec_col * LJ + vir_pick
    shape = (execs, N_COL, CAP, JPER)
    occ_global = jnp.broadcast_to(occ_global, shape).reshape(execs, -1)
    k_global = jnp.broadcast_to(k_global, shape).reshape(execs, -1)
    vir_global = jnp.broadcast_to(vir_global, shape).reshape(execs, -1)
    amp_id = occ_global * (LJ * N_COL) + vir_global
    int_id = vir_global * (KC * N_COL) + k_global
    res_id = occ_global * (KC * N_COL) + k_global
    stacked = jnp.stack([amp_id, int_id, res_id], axis=1)
    order_keys = jax.random.split(key_order, execs)
    orders = jax.vmap(lambda k: jax.random.permutation(k, TRIP_DEV))(order_keys).astype(jnp.int32)
    stacked = jnp.take_along_axis(stacked, orders[:, None, :], axis=2)
    return stacked.reshape(N_ROW, N_COL, 3, TRIP_DEV).astype(jnp.int32)


def level_of(own_key, extent, cuts, low, top_value):
    def one(axis_at, parts):
        heights = jax.random.uniform(jax.random.fold_in(jax.random.fold_in(own_key, 6), axis_at), (parts,), jnp.float32, low / len(cuts), top_value / len(cuts))
        return jnp.repeat(jnp.exp(heights), extent[axis_at] // parts).reshape((-1,) + (1,) * (len(extent) - axis_at - 1))

    level = one(*cuts[0])
    for cut in cuts[1:]:
        level = level * one(*cut)
    return level


def gaussian(own_key, shape, scale, reach, cuts=(), kind=jnp.bfloat16):
    values = scale * jax.random.normal(own_key, shape, jnp.float32)
    if cuts:
        values = values * level_of(own_key, shape, cuts, -0.22, 0.18)
    return jnp.clip(values, -reach, reach).astype(kind)


def setup_inputs(seed: int = 0) -> dict:
    seeds = jax.random.split(jax.random.key(seed), 5)
    return {
        "amp_tiles": gaussian(seeds[0], (MI_T, MJ_T, TILE, TILE), 1.0, 6.0, ((0, 8), (1, 16)), jnp.float32),
        "int_tiles": gaussian(seeds[1], (MJ_T, MK, TILE, TILE), (TILE * CAP * JPER * N_COL // (LI * KC)) ** -0.5, 0.125, ((0, 16), (1, 8)), jnp.float32),
        "resid_init": gaussian(seeds[2], (MI_T, MK, TILE, TILE), 1.0, 6.0, ((0, 8), (1, 16)), jnp.float32),
        "triples": draw_triples(jax.random.fold_in(seeds[4], 71), 0),
    }


def reference(amp_tiles, int_tiles, resid_init, triples):
    all_j = amp_tiles.shape[1]
    all_k = int_tiles.shape[1]
    amp_ids = triples[:, :, 0, :].reshape(-1)
    int_ids = triples[:, :, 1, :].reshape(-1)
    res_ids = triples[:, :, 2, :].reshape(-1)
    amp_row = amp_ids // all_j
    amp_col = amp_ids % all_j
    int_row = int_ids // all_k
    int_col = int_ids % all_k
    res_row = res_ids // all_k
    res_col = res_ids % all_k
    block = 64

    def add_block(partial_value, pieces):
        arow, acol, irow, icol, rrow, rcol = pieces
        left = amp_tiles[arow, acol]
        right = int_tiles[irow, icol]
        products = jnp.einsum("bxy,byz->bxz", left, right, precision=lax.Precision.HIGHEST, preferred_element_type=jnp.float32)
        return partial_value.at[rrow, rcol].add(products), None

    pieces = tuple(v.reshape(-1, block) for v in (amp_row, amp_col, int_row, int_col, res_row, res_col))
    result, _ = lax.scan(add_block, resid_init.astype(jnp.float32), pieces)
    return result
```

```python
import functools

import jax
import jax.numpy as jnp
from jax import lax
from jax.experimental import pallas as pl
from jax.experimental.pallas import tpu as pltpu
from jax.sharding import Mesh, PartitionSpec as P

SIZE = {"z": 4, "c": 2, "y": 4, "x": 4}


def shift(t, axis, s):
    n = SIZE[axis]
    return lax.ppermute(t, axis, [(i, (i + s) % n) for i in range(n)])


def split_kernel(a_ref, o_ref):
    a = a_ref[0]
    w = a.shape[1]
    hi = a.astype(jnp.bfloat16)
    lo = (a - hi.astype(jnp.float32)).astype(jnp.bfloat16)
    o_ref[0, :, :w] = hi
    o_ref[0, :, w : 2 * w] = lo
    o_ref[0, :, 2 * w :] = hi


def split_amp(a):
    n, w, _ = a.shape
    return pl.pallas_call(
        split_kernel,
        grid=(n,),
        in_specs=[pl.BlockSpec((1, w, w), lambda g: (g, 0, 0))],
        out_specs=pl.BlockSpec((1, w, 3 * w), lambda g: (g, 0, 0)),
        out_shape=jax.ShapeDtypeStruct((n, w, 3 * w), jnp.bfloat16),
        cost_estimate=pl.CostEstimate(flops=0, bytes_accessed=n * w * w * 10, transcendentals=0),
        name="split_amp",
    )(a)


def contract_kernel(meta_ref, a_ref, p_ref, r_ref, l_ref, f_ref, g_ref, o_ref, b_ref):
    step = pl.program_id(0)
    w = p_ref.shape[1]
    ka = lax.rem(meta_ref[128] + jnp.where(step == 1, 3, jnp.where(step == 2, 1, jnp.where(step == 3, 2, 0))), 4)

    def load(jx, b):
        hi = b.astype(jnp.bfloat16)
        lo = (b - hi.astype(jnp.float32)).astype(jnp.bfloat16)
        b_ref[jx, :w] = hi
        b_ref[jx, w : 2 * w] = hi
        b_ref[jx, 2 * w :] = lo

    for s, piece in enumerate((p_ref, r_ref, l_ref)):
        @pl.when(step == s)
        def _():
            for jx in range(4):
                load(jx, piece[jx])

    @pl.when(step == 3)
    def _():
        for jx in range(2):
            load(jx, f_ref[jx])
            load(jx + 2, g_ref[jx])

    o_ref[...] = jnp.zeros_like(o_ref)
    for i in range(4):
        for jx in range(4):
            @pl.when(meta_ref[ka * 16 + jx * 4 + i] != 0)
            def _():
                o_ref[i] += jnp.dot(a_ref[jx * 4 + i], b_ref[jx], preferred_element_type=jnp.float32)


def contract(meta, a3, pieces):
    w = a3.shape[1]
    full = lambda t: pl.BlockSpec(t.shape, lambda g, m: (0,) * t.ndim)
    order = lambda g, m: lax.rem(m[128] + jnp.where(g == 1, 3, jnp.where(g == 2, 1, jnp.where(g == 3, 2, 0))), 4)
    return pl.pallas_call(
        contract_kernel,
        grid_spec=pltpu.PrefetchScalarGridSpec(
            num_scalar_prefetch=1,
            grid=(4,),
            in_specs=[full(a3)] + [full(t) for t in pieces],
            out_specs=pl.BlockSpec((4, w, w), lambda g, m: (order(g, m), 0, 0)),
            scratch_shapes=[pltpu.VMEM((4, 3 * w, w), jnp.bfloat16)],
        ),
        out_shape=jax.ShapeDtypeStruct((16, w, w), jnp.float32),
        compiler_params=pltpu.CompilerParams(vmem_limit_bytes=50 * 1024 * 1024),
        cost_estimate=pl.CostEstimate(flops=16 * 6 * w**3, bytes_accessed=14 * 2**20, transcendentals=0),
        name="contract",
    )(meta, a3, *pieces)


def on_device(amp, integ, resid, triples):
    w = amp.shape[-1]
    z = lax.axis_index("z")
    c = lax.axis_index("c")
    x = lax.axis_index("x")

    def joined(mine, other):
        return jnp.where(c == 0, jnp.concatenate([mine, other]), jnp.concatenate([other, mine]))

    mine = lax.dynamic_index_in_dim(integ, c, 0, keepdims=False)
    other = shift(lax.dynamic_index_in_dim(integ, 1 - c, 0, keepdims=False), "c", 1)
    a_mine = lax.dynamic_index_in_dim(amp, c, 1, keepdims=False)
    a_other = shift(lax.dynamic_index_in_dim(amp, 1 - c, 1, keepdims=False), "c", 1)
    a_all = lax.all_gather(joined(a_mine, a_other), "x", axis=0, tiled=True)
    a3 = split_amp(a_all)

    tri = triples[0, 0]
    both = jnp.stack([tri, shift(tri, "c", 1)])
    lists = jnp.stack([both, shift(both, "x", 1), shift(both, "x", 2), shift(both, "x", 3)])
    amp_ids = lists[:, :, 0].reshape(-1)
    int_ids = lists[:, :, 1].reshape(-1)
    i = amp_ids // 32 - 4 * z
    j = amp_ids % 32
    k = int_ids % 32
    listed = (j % 2 == c) & ((k // 2) % 4 == x)
    slot = ((k % 2 * 4 + k // 8) * 4 + (j // 2) % 4) * 4 + i
    place = lax.broadcasted_iota(jnp.int32, (128, amp_ids.shape[0]), 0)
    mask = jnp.sum(((place == slot[None]) & listed[None]).astype(jnp.int32), axis=1)

    mine = mine.reshape(2, 2, w, w)
    other = other.reshape(2, 2, w, w)
    held = [lax.all_to_all(joined(mine[:, kp], other[:, kp]), "x", 0, 0, tiled=True) for kp in range(2)]
    right = [None, None]
    left = [None, None]
    sums = []
    for kp in range(2):
        right[kp] = shift(held[kp], "z", 1)
        left[kp] = shift(held[kp], "z", -1)
        if kp == 0:
            right[0], left[0], held[1] = lax.optimization_barrier((right[0], left[0], held[1]))
        far_a = shift(right[kp][:2], "z", 1)
        far_b = shift(left[kp][2:], "z", -1)
        meta = jnp.concatenate([mask.reshape(2, 64)[kp], jnp.zeros((64,), jnp.int32), z[None]])
        part = contract(meta, a3, (held[kp], right[kp], left[kp], far_a, far_b))
        sums.append(lax.psum_scatter(part, ("y", "c"), scatter_dimension=0, tiled=True))
    return resid + jnp.stack(sums, axis=1)


def solution(mesh):
    fine = Mesh(mesh.devices.reshape(4, 2, 4, 4), ("z", "c", "y", "x"))
    row, col = ("z", "c"), ("y", "x")
    return jax.shard_map(
        on_device,
        mesh=fine,
        in_specs=(P(row, col), P(col, row), P(row, col), P(row, col)),
        out_specs=P(row, col),
        check_vma=False,
    )
```

```python
import jax
import jax.numpy as jnp
from jax import lax
from jax.experimental import pallas as pl
from jax.experimental.pallas import tpu as pltpu
from jax.sharding import Mesh, PartitionSpec as P

NAMES = ("z", "c", "y", "x")
MIB = 1024 * 1024


def device(z, c, y, x):
    return ((z * 2 + c) * 4 + y) * 4 + x


EVERY = [(z, c, y, x) for z in range(4) for c in range(2) for y in range(4) for x in range(4)]


def move(t, target, keep=lambda *d: True):
    return lax.ppermute(t, NAMES, [(device(*d), device(*target(*d))) for d in EVERY if keep(*d)])


def along_z(t, s):
    return move(t, lambda z, c, y, x: ((z + s) % 4, c, y, x))


def over_core(t):
    return move(t, lambda z, c, y, x: (z, 1 - c, y, x))


def exchange(t, s):
    return move(t, lambda z, c, y, x: (z, c, y, (x + s) % 4) if c == 0 else (z, c, (y + s) % 4, x))


def reduce_to(t, s):
    return move(t, lambda z, c, y, x: (z, c, (y + s) % 4, x) if c == 0 else (z, c, y, (x + s) % 4))


def halves(a):
    hi = a.astype(jnp.bfloat16)
    return hi, (a - hi.astype(jnp.float32)).astype(jnp.bfloat16)


def split_kernel(a_ref, r_ref, l_ref, fa_ref, fb_ref, o_ref):
    w = a_ref.shape[-1]

    def put(s, a):
        hi, lo = halves(a)
        o_ref[s, 0, :, :w] = hi
        o_ref[s, 0, :, w : 2 * w] = lo
        o_ref[s, 0, :, 2 * w :] = hi

    put(0, a_ref[0])
    put(1, r_ref[0])
    put(3, l_ref[0])

    @pl.when(pl.program_id(0) < 2)
    def _():
        put(2, fa_ref[0])

    @pl.when(pl.program_id(0) >= 2)
    def _():
        put(2, fb_ref[0])


def split_amp(a, r, l, fa, fb):
    w = a.shape[-1]
    tile = lambda f: pl.BlockSpec((1, w, w), lambda g: (f(g), 0, 0))
    same = tile(lambda g: g)
    return pl.pallas_call(
        split_kernel,
        grid=(4,),
        in_specs=[same, same, same, tile(lambda g: jnp.minimum(g, 1)), tile(lambda g: jnp.maximum(g - 2, 0))],
        out_specs=pl.BlockSpec((4, 1, w, 3 * w), lambda g: (0, g, 0, 0)),
        out_shape=jax.ShapeDtypeStruct((4, 4, w, 3 * w), jnp.bfloat16),
        compiler_params=pltpu.CompilerParams(vmem_limit_bytes=12 * MIB),
        cost_estimate=pl.CostEstimate(flops=0, bytes_accessed=10 * MIB, transcendentals=0),
        name="split_amp",
    )(a, r, l, fa, fb)


def source_of(step, z):
    return lax.rem(z + jnp.where(step == 1, 3, jnp.where(step == 2, 1, jnp.where(step == 3, 2, 0))), 4)


def make_contract_kernel(kp):
    def kernel(meta_ref, a_ref, own, own_r, own_l, own_fa, own_fb, rest, rest_r, rest_l, rest_fa, rest_fb, *outs):
        outs, (b_ref, acc_ref) = outs[:4], outs[4:]
        step = pl.program_id(0)
        w = b_ref.shape[2]
        h = w // 2
        ka = source_of(step, meta_ref[64])

        def load(s, b, at=0):
            n = b.shape[0]
            hi, lo = halves(b)
            b_ref[s, at : at + n] = hi
            b_ref[s, w + at : w + at + n] = hi
            b_ref[s, 2 * w + at : 2 * w + at + n] = lo

        for at, (mine, others) in enumerate(((own, rest), (own_r, rest_r), (own_l, rest_l))):
            @pl.when(step == at)
            def _():
                load(0, mine[kp])
                for s in range(3):
                    load(s + 1, others[s])

        @pl.when(step == 3)
        def _():
            for part, (mine, others) in enumerate(((own_fa, rest_fa), (own_fb, rest_fb))):
                load(0, mine[3, kp * h : kp * h + h], part * h)
                for s in range(3):
                    load(s + 1, others[s], part * h)

        acc_ref[...] = jnp.zeros_like(acc_ref)
        for i in range(4):
            for s in range(4):
                @pl.when(meta_ref[ka * 16 + s * 4 + i] != 0)
                def _():
                    acc_ref[i] += jnp.dot(a_ref[s, i], b_ref[s], preferred_element_type=jnp.float32)
        away = lax.rem(ka + 4 - meta_ref[65], 4)
        for s in range(4):
            @pl.when(away == s)
            def _():
                outs[s][...] = acc_ref[...]

    return kernel


def contract(kp, meta, a3, own, rest):
    w = a3.shape[2]
    full = lambda t: pl.BlockSpec(t.shape, lambda g, m: (0,) * t.ndim)
    out = jax.ShapeDtypeStruct((4, w, w), jnp.float32)
    return pl.pallas_call(
        make_contract_kernel(kp),
        grid_spec=pltpu.PrefetchScalarGridSpec(
            num_scalar_prefetch=1,
            grid=(4,),
            in_specs=[full(t) for t in (a3,) + own + rest],
            out_specs=[full(out)] * 4,
            scratch_shapes=[pltpu.VMEM((4, 3 * w, w), jnp.bfloat16), pltpu.VMEM((4, w, w), jnp.float32)],
        ),
        out_shape=[out] * 4,
        compiler_params=pltpu.CompilerParams(vmem_limit_bytes=40 * MIB),
        cost_estimate=pl.CostEstimate(flops=16 * 6 * w**3, bytes_accessed=14 * MIB, transcendentals=0),
        name="contract",
    )(meta, a3, *own, *rest)


def on_device(amp, integ, resid, triples):
    w = amp.shape[-1]
    h = w // 2
    z, c, y, x = (lax.axis_index(n) for n in NAMES)
    upos = jnp.where(c == 0, x, y)
    vpos = jnp.where(c == 0, y, x)

    def joined(mine, other):
        return jnp.where(c == 0, jnp.concatenate([mine, other]), jnp.concatenate([other, mine]))

    mine = lax.dynamic_index_in_dim(integ, c, 0, keepdims=False)
    other = over_core(lax.dynamic_index_in_dim(integ, 1 - c, 0, keepdims=False))
    pairs = joined(mine.reshape(2, 2, w, w), other.reshape(2, 2, w, w))
    tiles = [lax.dynamic_index_in_dim(pairs, lax.rem(upos + s, 4), 0, keepdims=False) for s in range(4)]
    own = tiles[0]
    own_r, own_l = along_z(own, 1), along_z(own, -1)
    came = [exchange(tiles[s], s) for s in (1, 2, 3)]
    rest = [jnp.stack([t[kp] for t in came]) for kp in range(2)]

    a_mine = lax.dynamic_index_in_dim(amp, c, 1, keepdims=False)
    a_other = over_core(lax.dynamic_index_in_dim(amp, 1 - c, 1, keepdims=False))
    a0 = joined(a_mine, a_other)
    a0, tri, rest[0], rest[1] = lax.optimization_barrier((a0, triples[0, 0], rest[0], rest[1]))
    a_r, a_l = exchange(a0, 1), exchange(a0, -1)
    a3 = split_amp(a0, a_r, a_l, exchange(a_r[:2], 1), exchange(a_l[2:], -1))

    two_r = along_z(jnp.concatenate([rest[0], own_r[:, :h].reshape(1, w, w)]), 1)
    two_l = along_z(jnp.concatenate([rest[0], own_l[:, h:].reshape(1, w, w)]), -1)
    two_r, two_l, rest[1] = lax.optimization_barrier((two_r, two_l, rest[1]))
    far0 = along_z(two_r[:3, :h], 1), along_z(two_l[:3, h:], -1)
    rest1_r, rest1_l = along_z(rest[1], 1), along_z(rest[1], -1)
    far1 = along_z(rest1_r[:, :h], 1), along_z(rest1_l[:, h:], -1)

    both = jnp.stack([tri, over_core(tri)])
    lists = jnp.stack([both, exchange(both, 1), exchange(both, 2), exchange(both, 3)])
    amp_ids = lists[:, :, 0].reshape(-1)
    int_ids = lists[:, :, 1].reshape(-1)
    i = amp_ids // 32 - 4 * z
    j = amp_ids % 32
    k = int_ids % 32
    listed = (j % 2 == c) & ((k // 2) % 4 == upos)
    s = (upos - jnp.where(c == 0, (j // 2) % 4, j // 8)) % 4
    slot = ((k % 2 * 4 + k // 8) * 4 + s) * 4 + i
    place = lax.broadcasted_iota(jnp.int32, (128, amp_ids.shape[0]), 0)
    mask = jnp.sum(((place == slot[None]) & listed[None]).astype(jnp.int32), axis=1)
    where = jnp.stack([z, vpos])

    outs = []
    pieces = ((rest[0], two_r, two_l) + far0, (rest[1], rest1_r, rest1_l) + far1)
    for kp in range(2):
        meta = jnp.concatenate([mask[64 * kp : 64 * kp + 64], where])
        parts = contract(kp, meta, a3, (own, own_r, own_l, two_r, two_l), pieces[kp])
        total = parts[0]
        for s in (1, 2, 3):
            total = total + reduce_to(parts[s], s)
        lower, upper = total[:2], total[2:]
        swapped = move(
            jnp.where(c == 0, upper, lower), lambda z, c, y, x: (z, 1, y, x) if c == 0 else (z, 0, x, y)
        )
        turned = move(upper, lambda z, c, y, x: (z, 1, x, y), lambda z, c, y, x: c == 1)
        outs.append(resid[:, kp] + swapped + jnp.where(c == 0, lower, turned))
    return jnp.stack(outs, axis=1)


def solution(mesh):
    fine = Mesh(mesh.devices.reshape(4, 2, 4, 4), NAMES)
    row, col = ("z", "c"), ("y", "x")
    return jax.shard_map(
        on_device,
        mesh=fine,
        in_specs=(P(row, col), P(col, row), P(row, col), P(row, col)),
        out_specs=P(row, col),
        check_vma=False,
    )
```

```python
import jax
import jax.numpy as jnp
from jax import lax
from jax.experimental import pallas as pl
from jax.experimental.pallas import tpu as pltpu
from jax.sharding import Mesh, PartitionSpec as P

NAMES = ("z", "c", "y", "x")
SIZE = {"z": 4, "c": 2, "y": 4, "x": 4}
MIB = 1024 * 1024
CHUNKS = ((0, 0, 256), (1, 0, 128), (1, 128, 128))


def shift(t, axis, s):
    n = SIZE[axis]
    return lax.ppermute(t, axis, [(i, (i + s) % n) for i in range(n)])


def halves(a):
    hi = a.astype(jnp.bfloat16)
    return hi, (a - hi.astype(jnp.float32)).astype(jnp.bfloat16)


def split_kernel(a_ref, r_ref, l_ref, fa_ref, fb_ref, o_ref):
    w = a_ref.shape[-1]

    def put(s, ref):
        for il in range(2):
            hi, lo = halves(ref[0, il * w : il * w + w])
            o_ref[s, il, :, :w] = hi
            o_ref[s, il, :, w : 2 * w] = lo
            o_ref[s, il, :, 2 * w :] = hi

    put(0, a_ref)
    put(1, r_ref)
    put(3, l_ref)

    @pl.when(pl.program_id(0) == 0)
    def _():
        put(2, fa_ref)

    @pl.when(pl.program_id(0) == 1)
    def _():
        put(2, fb_ref)


def split_amp(a, r, l, fa, fb):
    rows, w = a.shape[1:]
    each = pl.BlockSpec((1, rows, w), lambda g: (g, 0, 0))
    only = pl.BlockSpec((1, rows, w), lambda g: (0, 0, 0))
    return pl.pallas_call(
        split_kernel,
        grid=(2,),
        in_specs=[each, each, each, only, only],
        out_specs=pl.BlockSpec((4, 2, w, 3 * w), lambda g: (0, g, 0, 0)),
        out_shape=jax.ShapeDtypeStruct((4, 4, w, 3 * w), jnp.bfloat16),
        compiler_params=pltpu.CompilerParams(vmem_limit_bytes=18 * MIB),
        cost_estimate=pl.CostEstimate(flops=0, bytes_accessed=10 * MIB, transcendentals=0),
        name="split_amp",
    )(a, r, l, fa, fb)


def make_contract_kernel(kp, first, width):
    def kernel(flag_ref, a_ref, own, own_r, own_l, own_fa, own_fb, rest, rest_r, rest_l, rest_fa, rest_fb,
               mine_ref, other_ref, b_ref):
        w = a_ref.shape[2]
        h = w // 2
        columns = slice(first, first + width)

        def load(s, b, at=0):
            n = b.shape[0]
            hi, lo = halves(b)
            b_ref[s, at : at + n] = hi
            b_ref[s, w + at : w + at + n] = hi
            b_ref[s, 2 * w + at : 2 * w + at + n] = lo

        z, c, y = flag_ref[128], flag_ref[129], flag_ref[130]

        @pl.loop(0, 4)
        def _(step):
            ka = lax.rem(z + jnp.where(step == 1, 3, jnp.where(step == 2, 1, jnp.where(step == 3, 2, 0))), 4)
            for at, (mine, others) in enumerate(((own, rest), (own_r, rest_r), (own_l, rest_l))):
                @pl.when(step == at)
                def _():
                    load(0, mine[kp, :, columns])
                    for s in range(3):
                        load(s + 1, others[s])

            @pl.when(step == 3)
            def _():
                for part, (mine, others) in enumerate(((own_fa, rest_fa), (own_fb, rest_fb))):
                    load(0, mine[kp, :, columns], part * h)
                    for s in range(3):
                        load(s + 1, others[s], part * h)

            away = lax.rem(ka + 4 - y, 4)
            for out, core in ((mine_ref, c), (other_ref, 1 - c)):
                for il in range(2):
                    out[away, il] = jnp.zeros((w, width), jnp.float32)
                    for s in range(4):
                        @pl.when(flag_ref[(s * 2 + core) * 16 + kp * 8 + ka * 2 + il] != 0)
                        def _():
                            out[away, il] += jnp.dot(
                                a_ref[s, 2 * core + il], b_ref[s], preferred_element_type=jnp.float32
                            )

    return kernel


def contract(chunk, flags, a3, own, rest):
    w = a3.shape[2]
    width = chunk[2]
    inside = pl.BlockSpec(memory_space=pltpu.VMEM)
    out = jax.ShapeDtypeStruct((4, 2, w, width), jnp.float32)
    return pl.pallas_call(
        make_contract_kernel(*chunk),
        in_specs=[pl.BlockSpec(memory_space=pltpu.SMEM)] + [inside] * 11,
        out_specs=[inside, inside],
        scratch_shapes=[pltpu.VMEM((4, 3 * w, width), jnp.bfloat16)],
        out_shape=[out, out],
        compiler_params=pltpu.CompilerParams(vmem_limit_bytes=28 * MIB),
        cost_estimate=pl.CostEstimate(flops=16 * 6 * w * w * width, bytes_accessed=8 * MIB, transcendentals=0),
        name="contract",
    )(flags, a3, *own, *rest)


def on_device(amp, integ, resid, triples):
    w = amp.shape[-1]
    h = w // 2
    z, c, y, x = (lax.axis_index(n) for n in NAMES)

    def joined(mine, other):
        return jnp.where(c == 0, jnp.stack([mine, other]), jnp.stack([other, mine]))

    mine = lax.dynamic_index_in_dim(integ, c, 0, keepdims=False)
    other = shift(lax.dynamic_index_in_dim(integ, 1 - c, 0, keepdims=False), "c", 1)
    pairs = joined(mine, other).reshape(4, 2, w, w)
    tiles = [lax.dynamic_index_in_dim(pairs, lax.rem(x + s, 4), 0, keepdims=False) for s in range(4)]
    own = tiles[0]
    own_r, own_l = shift(own, "z", 1), shift(own, "z", -1)
    came = [[shift(tiles[s][kp], "x", s) for s in (1, 2, 3)] for kp in range(2)]
    rest = [jnp.stack([t[:, f : f + n] for t in came[kp]]) for kp, f, n in CHUNKS]

    tri = triples[0, 0]
    i = tri[0] // 32
    j = tri[0] % 32
    k = tri[1] % 32
    slot = (((j % 2 * 4 + (k // 2) % 4) * 2 + k % 2) * 4 + k // 8) * 2 + i % 2
    place = lax.broadcasted_iota(jnp.int32, (32, w), 1)
    listed = jnp.sum((place == slot[:, None]).astype(jnp.float32), axis=0, keepdims=True)
    listed = jnp.broadcast_to(listed, (8, w))

    def with_flags(parity):
        tile = lax.dynamic_index_in_dim(amp, parity, 1, keepdims=False)
        return jnp.concatenate([tile.reshape(2 * w, w), listed])

    a0 = joined(with_flags(c), shift(with_flags(1 - c), "c", 1))
    a0, rest[0] = lax.optimization_barrier((a0, rest[0]))
    a_r, a_l = shift(a0, "x", 1), shift(a0, "x", -1)
    a_fa, a_fb = shift(a_r[:1], "x", 1), shift(a_l[1:], "x", -1)
    a3 = split_amp(a0, a_r, a_l, a_fa, a_fb)
    rows = jnp.stack([a0[:, 2 * w, :128], a_r[:, 2 * w, :128],
                      jnp.concatenate([a_fa[:, 2 * w, :128], a_fb[:, 2 * w, :128]]), a_l[:, 2 * w, :128]])
    flags = lax.dynamic_index_in_dim(rows.reshape(4, 2, 8, 16), c * 4 + x, 2, keepdims=False)
    flags = jnp.concatenate([flags.reshape(-1).astype(jnp.int32), jnp.stack([z, c, y])])

    own_fa, own_fb = shift(own_r[:, :h], "z", 1), shift(own_l[:, h:], "z", -1)
    right, left, far = [], [], []
    for n in range(len(CHUNKS)):
        if n:
            right[-1], left[-1], rest[n] = lax.optimization_barrier((right[-1], left[-1], rest[n]))
            far.append((shift(right[-1][:, :h], "z", 1), shift(left[-1][:, h:], "z", -1)))
        right.append(shift(rest[n], "z", 1))
        left.append(shift(rest[n], "z", -1))
    far.append((shift(right[-1][:, :h], "z", 1), shift(left[-1][:, h:], "z", -1)))

    outs = []
    for n, chunk in enumerate(CHUNKS):
        kp, first, width = chunk
        held, away = contract(
            chunk, flags, a3, (own, own_r, own_l, own_fa, own_fb), (rest[n], right[n], left[n]) + far[n]
        )
        part = held + shift(away, "c", 1)
        total = resid[:, kp, :, first : first + width] + part[0]
        for s in (1, 2, 3):
            total = total + shift(part[s], "y", s)
        outs.append(total)
    return jnp.stack([outs[0], jnp.concatenate(outs[1:], axis=-1)], axis=1)


def solution(mesh):
    fine = Mesh(mesh.devices.reshape(4, 2, 4, 4), NAMES)
    row, col = ("z", "c"), ("y", "x")
    return jax.shard_map(
        on_device,
        mesh=fine,
        in_specs=(P(row, col), P(col, row), P(row, col), P(row, col)),
        out_specs=P(row, col),
        check_vma=False,
    )
```

```python
import jax
import jax.numpy as jnp
from jax import lax
from jax.experimental import pallas as pl
from jax.experimental.pallas import tpu as pltpu
from jax.sharding import Mesh, PartitionSpec as P

NAMES = ("z", "c", "y", "x")
SIZE = {"z": 4, "c": 2, "y": 4, "x": 4}
MIB = 1024 * 1024
CHUNKS = ((0, (0,)), (0, (1,)), (1, (0, 1)))


def shift(t, axis, s):
    n = SIZE[axis]
    return lax.ppermute(t, axis, [(i, (i + s) % n) for i in range(n)])


def halves(a):
    hi = a.astype(jnp.bfloat16)
    return hi, (a - hi.astype(jnp.float32)).astype(jnp.bfloat16)


def split_kernel(a_ref, o_ref):
    w = a_ref.shape[-1]
    for c in range(2):
        hi, lo = halves(a_ref[0, c, :w])
        o_ref[0, c, :, :w] = hi
        o_ref[0, c, :, w : 2 * w] = lo
        o_ref[0, c, :, 2 * w :] = hi


def split_amp(a):
    rows, w = a.shape[2:]
    return pl.pallas_call(
        split_kernel,
        grid=(4,),
        in_specs=[pl.BlockSpec((1, 2, rows, w), lambda g: (g, 0, 0, 0))],
        out_specs=pl.BlockSpec((1, 2, w, 3 * w), lambda g: (g, 0, 0, 0)),
        out_shape=jax.ShapeDtypeStruct((4, 2, w, 3 * w), jnp.bfloat16),
        compiler_params=pltpu.CompilerParams(vmem_limit_bytes=8 * MIB),
        cost_estimate=pl.CostEstimate(flops=0, bytes_accessed=5 * MIB, transcendentals=0),
        name="split_amp",
    )(a)


def make_contract_kernel(kp, rows):
    def kernel(flag_ref, *refs):
        amps, refs = refs[: len(rows)], refs[len(rows) :]
        own, own_r, own_l, rest, two_r, two_l, fa, fb, mine_ref, other_ref, b_ref = refs
        w = amps[0].shape[2]
        h = w // 2

        def load(s, b, at=0):
            n = b.shape[0]
            hi, lo = halves(b)
            b_ref[s, at : at + n] = hi
            b_ref[s, w + at : w + at + n] = hi
            b_ref[s, 2 * w + at : 2 * w + at + n] = lo

        z, c, x = flag_ref[128], flag_ref[129], flag_ref[130]

        @pl.loop(0, 4)
        def _(step):
            ka = lax.rem(z + jnp.where(step == 1, 3, jnp.where(step == 2, 1, jnp.where(step == 3, 2, 0))), 4)
            for at, (mine, others) in enumerate(((own, rest), (own_r, two_r), (own_l, two_l))):
                @pl.when(step == at)
                def _():
                    load(0, mine[kp])
                    for s in range(3):
                        load(s + 1, others[s])

            @pl.when(step == 3)
            def _():
                for part, ref in enumerate((fa, fb)):
                    for s in range(4):
                        load(s, ref[s], part * h)

            for out, core in ((mine_ref, c), (other_ref, 1 - c)):
                for n, il in enumerate(rows):
                    out[ka, n] = jnp.zeros((w, w), jnp.float32)
                    for s in range(4):
                        jx = lax.rem(x + s, 4)

                        @pl.when(flag_ref[(jx * 2 + core) * 16 + kp * 8 + ka * 2 + il] != 0)
                        def _():
                            out[ka, n] += jnp.dot(amps[n][jx, core], b_ref[s], preferred_element_type=jnp.float32)

    return kernel


def contract(chunk, flags, amps, pieces):
    kp, rows = chunk
    w = amps[0].shape[2]
    inside = pl.BlockSpec(memory_space=pltpu.VMEM)
    out = jax.ShapeDtypeStruct((4, len(rows), w, w), jnp.float32)
    return pl.pallas_call(
        make_contract_kernel(kp, rows),
        in_specs=[pl.BlockSpec(memory_space=pltpu.SMEM)] + [inside] * (len(amps) + len(pieces)),
        out_specs=[inside, inside],
        scratch_shapes=[pltpu.VMEM((4, 3 * w, w), jnp.bfloat16)],
        out_shape=[out, out],
        compiler_params=pltpu.CompilerParams(vmem_limit_bytes=28 * MIB),
        cost_estimate=pl.CostEstimate(flops=16 * 6 * w**3, bytes_accessed=8 * MIB, transcendentals=0),
        name="contract",
    )(flags, *amps, *pieces)


def on_device(amp, integ, resid, triples):
    w = amp.shape[-1]
    h = w // 2
    z, c, y, x = (lax.axis_index(n) for n in NAMES)

    def joined(mine, other):
        return jnp.where(c == 0, jnp.stack([mine, other]), jnp.stack([other, mine]))

    mine = lax.dynamic_index_in_dim(integ, c, 0, keepdims=False)
    other = shift(lax.dynamic_index_in_dim(integ, 1 - c, 0, keepdims=False), "c", 1)
    pairs = joined(mine, other).reshape(4, 2, w, w)
    own = lax.dynamic_index_in_dim(pairs, x, 0, keepdims=False)
    own_r, own_l = shift(own, "z", 1), shift(own, "z", -1)

    def others(kp):
        held = lax.all_to_all(pairs[:, kp], "x", 0, 0, tiled=True)
        return lax.dynamic_slice_in_dim(jnp.concatenate([held, held]), x + 1, 3, 0)

    rest = [others(0), others(1)]

    tri = triples[0, 0]
    i = tri[0] // 32
    j = tri[0] % 32
    k = tri[1] % 32
    slot = (((j % 2 * 4 + (k // 2) % 4) * 2 + k % 2) * 4 + k // 8) * 2 + i % 2
    place = lax.broadcasted_iota(jnp.int32, (32, w), 1)
    listed = jnp.sum((place == slot[:, None]).astype(jnp.float32), axis=0, keepdims=True)
    listed = jnp.broadcast_to(listed, (8, w))

    def with_flags(parity):
        tile = lax.dynamic_index_in_dim(amp, parity, 1, keepdims=False)
        return jnp.concatenate([tile, jnp.broadcast_to(listed[None], (2, 8, w))], axis=1)

    a0 = joined(with_flags(c), shift(with_flags(1 - c), "c", 1))
    gathered = [lax.all_gather(a0[:, il], "x") for il in range(2)]
    amps = [split_amp(g) for g in gathered]
    flags = gathered[0][:, :, w, :128].reshape(4, 2, 8, 16)
    flags = lax.dynamic_index_in_dim(flags, c * 4 + x, 2, keepdims=False)
    flags = jnp.concatenate([flags.reshape(-1).astype(jnp.int32), jnp.stack([z, c, x])])

    two_r = shift(jnp.concatenate([rest[0], own_r[:, :h].reshape(1, w, w)]), "z", 1)
    two_l = shift(jnp.concatenate([rest[0], own_l[:, h:].reshape(1, w, w)]), "z", -1)
    two_r, two_l, rest[1] = lax.optimization_barrier((two_r, two_l, rest[1]))
    far0 = shift(two_r[:3, :h], "z", 1), shift(two_l[:3, h:], "z", -1)
    rest1_r, rest1_l = shift(rest[1], "z", 1), shift(rest[1], "z", -1)
    far1 = shift(rest1_r[:, :h], "z", 1), shift(rest1_l[:, h:], "z", -1)
    own_fa, own_fb = two_r[3].reshape(2, h, w), two_l[3].reshape(2, h, w)

    def far(kp, fa, fb):
        return jnp.concatenate([own_fa[kp : kp + 1], fa]), jnp.concatenate([own_fb[kp : kp + 1], fb])

    pieces = ((rest[0], two_r, two_l) + far(0, *far0), (rest[1], rest1_r, rest1_l) + far(1, *far1))
    sums = []
    for kp, rows in CHUNKS:
        held, away = contract((kp, rows), flags, [amps[il] for il in rows], (own, own_r, own_l) + pieces[kp])
        part = held + shift(away, "c", 1)
        part, flags = lax.optimization_barrier((part, flags))
        part = lax.all_to_all(part, "y", 0, 0, tiled=True)
        sums.append(part[0] + part[1] + part[2] + part[3])
    return resid + jnp.stack([jnp.concatenate(sums[:2]), sums[2]], axis=1)


def solution(mesh):
    fine = Mesh(mesh.devices.reshape(4, 2, 4, 4), NAMES)
    row, col = ("z", "c"), ("y", "x")
    return jax.shard_map(
        on_device,
        mesh=fine,
        in_specs=(P(row, col), P(col, row), P(row, col), P(row, col)),
        out_specs=P(row, col),
        check_vma=False,
    )
```

```python
import jax
import jax.numpy as jnp
from jax import lax
from jax.experimental import pallas as pl
from jax.experimental.pallas import tpu as pltpu
from jax.sharding import Mesh, PartitionSpec as P

NAMES = ("z", "c", "y", "x")
SIZE = {"z": 4, "c": 2, "y": 4, "x": 4}
MIB = 1024 * 1024
CHUNKS = ((0, 0, 1), (0, 1, 1), (1, 0, 2))
BLOCK = 128


def shift(t, axis, s):
    n = SIZE[axis]
    return lax.ppermute(t, axis, [(i, (i + s) % n) for i in range(n)])


def halves(a):
    hi = a.astype(jnp.bfloat16)
    return hi, (a - hi.astype(jnp.float32)).astype(jnp.bfloat16)


def split_kernel(c_ref, a_ref, b_ref, o_ref):
    w = a_ref.shape[-1]
    for il, ref in enumerate((a_ref, b_ref)):
        for core in range(2):
            hi, lo = halves(ref[core])
            o_ref[0, 2 * core + il, :, :w] = hi
            o_ref[0, 2 * core + il, :, w : 2 * w] = lo
            o_ref[0, 2 * core + il, :, 2 * w :] = hi


def split_amp(c, a):
    w = a.shape[-1]
    tile = lambda il: pl.BlockSpec((2, w, w), lambda g, m: (g, 2 * il + m[0], 0))
    return pl.pallas_call(
        split_kernel,
        grid_spec=pltpu.PrefetchScalarGridSpec(
            num_scalar_prefetch=1,
            grid=(4,),
            in_specs=[tile(0), tile(1)],
            out_specs=pl.BlockSpec((1, 4, w, 3 * w), lambda g, m: (g, 0, 0, 0)),
        ),
        out_shape=jax.ShapeDtypeStruct((4, 4, w, 3 * w), jnp.bfloat16),
        compiler_params=pltpu.CompilerParams(vmem_limit_bytes=12 * MIB),
        cost_estimate=pl.CostEstimate(flops=0, bytes_accessed=10 * MIB, transcendentals=0),
        name="split_amp",
    )(c, a, a)


def make_contract_kernel(wide, places):
    def kernel(flag_ref, *refs):
        count = 1 + max(p[0] for step in places for p in step)
        pieces, refs = refs[:count], refs[count:]
        amp_ref, mine_ref, other_ref, a_ref, raw_ref, b_ref, sems = refs
        w = a_ref.shape[2]
        copies = []
        number = 0
        for step, wanted in enumerate(places):
            row = []
            for operand, first, rows, to in wanted:
                source = pieces[operand].at[pl.ds(first, rows)]
                row.append(pltpu.make_async_copy(source, raw_ref.at[step, pl.ds(to, rows)], sems.at[number]))
                number += 1
            copies.append(row)
        whole = pltpu.make_async_copy(amp_ref, a_ref, sems.at[number])
        for copy in copies[0]:
            copy.start()
        whole.start()
        for row in copies[1:]:
            for copy in row:
                copy.start()
        whole.wait()
        z, c, x = flag_ref[128], flag_ref[129], flag_ref[130]
        kp = flag_ref[131]
        for step, turn in enumerate((0, 3, 1, 2)):
            for copy in copies[step]:
                copy.wait()
            for s in range(4):
                for block in range(wide):
                    hi, lo = halves(raw_ref[step, (s * wide + block) * w : (s * wide + block + 1) * w])
                    columns = slice(block * BLOCK, block * BLOCK + BLOCK)
                    b_ref[s, :w, columns] = hi
                    b_ref[s, w : 2 * w, columns] = hi
                    b_ref[s, 2 * w :, columns] = lo
            ka = lax.rem(z + turn, 4)
            for out, core in ((mine_ref, c), (other_ref, 1 - c)):
                for il in range(2):
                    out[ka, il] = jnp.zeros(out.shape[2:], jnp.float32)

                    @pl.loop(0, 4)
                    def _(s):
                        jx = lax.rem(x + s, 4)

                        @pl.when(flag_ref[(jx * 2 + core) * 16 + kp * 8 + ka * 2 + il] != 0)
                        def _():
                            out[ka, il] += jnp.dot(
                                a_ref[jx, 2 * core + il], b_ref[s], preferred_element_type=jnp.float32
                            )

    return kernel


def contract(wide, flags, a3, pieces, places):
    w = a3.shape[2]
    inside = pl.BlockSpec(memory_space=pltpu.VMEM)
    outside = pl.BlockSpec(memory_space=pltpu.HBM)
    out = jax.ShapeDtypeStruct((4, 2, w, wide * BLOCK), jnp.float32)
    return pl.pallas_call(
        make_contract_kernel(wide, places),
        in_specs=[pl.BlockSpec(memory_space=pltpu.SMEM)] + [outside] * (len(pieces) + 1),
        out_specs=[inside, inside],
        scratch_shapes=[
            pltpu.VMEM(a3.shape, jnp.bfloat16),
            pltpu.VMEM((4, 4 * wide * w, BLOCK), jnp.float32),
            pltpu.VMEM((4, 3 * w, wide * BLOCK), jnp.bfloat16),
            pltpu.SemaphoreType.DMA((sum(len(p) for p in places) + 1,)),
        ],
        out_shape=[out, out],
        compiler_params=pltpu.CompilerParams(vmem_limit_bytes=24 * MIB),
        cost_estimate=pl.CostEstimate(flops=6 * wide * 10**9, bytes_accessed=4 * MIB, transcendentals=0),
        name="contract",
    )(flags, *pieces, a3)


def on_device(amp, integ, resid, triples):
    w = amp.shape[-1]
    h = w // 2
    z, c, y, x = (lax.axis_index(n) for n in NAMES)

    tri = triples[0, 0]
    i = tri[0] // 32
    j = tri[0] % 32
    k = tri[1] % 32
    slot = (((j % 2 * 4 + (k // 2) % 4) * 2 + k % 2) * 4 + k // 8) * 2 + i % 2
    place = lax.broadcasted_iota(jnp.int32, (32, w), 1)
    listed = jnp.sum((place == slot[:, None]).astype(jnp.float32), axis=0, keepdims=True)

    gathered = lax.all_gather(
        jnp.concatenate([amp.reshape(4 * w, w), jnp.broadcast_to(listed, (8, w))]), ("x", "c")
    )
    a3 = split_amp(c[None], gathered)
    flags = lax.dynamic_index_in_dim(gathered[:, 4 * w, :128].reshape(4, 2, 8, 16), c * 4 + x, 2, keepdims=False)
    flags = flags.reshape(-1).astype(jnp.int32)

    def blocked(t):
        return t.reshape(-1, w, 2, BLOCK).transpose(0, 2, 1, 3)

    mine = lax.dynamic_index_in_dim(integ, c, 0, keepdims=False)
    other = shift(lax.dynamic_index_in_dim(integ, 1 - c, 0, keepdims=False), "c", 1)
    pairs = jnp.where(c == 0, jnp.stack([mine, other]), jnp.stack([other, mine])).reshape(4, 2, w, w)
    own = blocked(lax.dynamic_index_in_dim(pairs, x, 0, keepdims=False)).reshape(-1, BLOCK)
    own, pairs = lax.optimization_barrier((own, pairs))
    own_r, own_l = shift(own, "z", 1), shift(own, "z", -1)
    rest = []
    for kp, first, blocks in CHUNKS:
        sent = pairs[:, kp, :, first * BLOCK : (first + blocks) * BLOCK]
        if not rest:
            held = jnp.stack([
                shift(lax.dynamic_index_in_dim(sent, lax.rem(x + 4 - s, 4), 0, keepdims=False), "x", -s)
                for s in (1, 2, 3)
            ])
        else:
            held = lax.all_to_all(sent, "x", 0, 0, tiled=True)
            held = lax.dynamic_slice_in_dim(jnp.concatenate([held, held]), x + 1, 3, 0)
        rest.append((blocked(held) if blocks == 2 else held).reshape(-1, BLOCK))

    def halved(right, left):
        right, left = right.reshape(-1, 2, h, BLOCK), left.reshape(-1, 2, h, BLOCK)
        return right[:, 0].reshape(-1, BLOCK), left[:, 1].reshape(-1, BLOCK)

    near = [(own_r, own_l)]
    pending = halved(own_r, own_l)
    for n in range(3):
        right, left = jnp.concatenate([rest[n], pending[0]]), jnp.concatenate([rest[n], pending[1]])
        if n == 2:
            right, left, flags = lax.optimization_barrier((right, left, flags))
        right, left = shift(right, "z", 1), shift(left, "z", -1)
        if n < 2:
            right, left, rest[n + 1] = lax.optimization_barrier((right, left, rest[n + 1]))
        near.append((right, left))
        body = rest[n].shape[0]
        pending = halved(right[:body], left[:body])
    near.append((shift(pending[0], "z", 1), shift(pending[1], "z", -1)))

    outs = []
    for n, (kp, first, blocks) in enumerate(CHUNKS):
        at = kp * 2 + first
        before = 0 if n == 2 else rest[n + 1].shape[0]
        pieces = [own, rest[n], own_r, near[n + 1][0], own_l, near[n + 1][1], *near[1], *near[n + 2]]
        places = [[(o, at * w, blocks * w, 0), (o + 1, 0, 3 * blocks * w, blocks * w)] for o in (0, 2, 4)]
        last = []
        for side in range(2):
            for t in range(4 * blocks):
                source = (6 + side, rest[0].shape[0] + (at + t) * h) if t < blocks else (
                    8 + side, before + (t - blocks) * h)
                last.append((*source, h, t * w + side * h))
        places.append(last)
        meta = jnp.concatenate([flags, jnp.stack([z, c, x, jnp.full_like(z, kp)])])
        held, away = contract(blocks, meta, a3, pieces, places)
        part = held + shift(away, "c", 1)
        part, flags = lax.optimization_barrier((part, flags))
        part = lax.all_to_all(part, "y", 0, 0, tiled=True)
        outs.append(part[0] + part[1] + part[2] + part[3])
        if n == 1:
            flags, outs[0] = lax.optimization_barrier((flags, outs[0]))
    return resid + jnp.stack([jnp.concatenate(outs[:2], axis=-1), outs[2]], axis=1)


def solution(mesh):
    fine = Mesh(mesh.devices.reshape(4, 2, 4, 4), NAMES)
    row, col = ("z", "c"), ("y", "x")
    return jax.shard_map(
        on_device,
        mesh=fine,
        in_specs=(P(row, col), P(col, row), P(row, col), P(row, col)),
        out_specs=P(row, col),
        check_vma=False,
    )
```

```python
import jax
import jax.numpy as jnp
from jax import lax
from jax.experimental import pallas as pl
from jax.experimental.pallas import tpu as pltpu
from jax.sharding import Mesh, PartitionSpec as P

NAMES = ("z", "c", "y", "x")
SIZE = {"z": 4, "c": 2, "y": 4, "x": 4}
MIB = 1024 * 1024

def shift(t, axis, s):
    n = SIZE[axis]
    return lax.ppermute(t, axis, [(i, (i + s) % n) for i in range(n)])


def halves(a):
    hi = a.astype(jnp.bfloat16)
    return hi, (a - hi.astype(jnp.float32)).astype(jnp.bfloat16)


def split_kernel(c_ref, a_ref, b_ref, o_ref):
    w = a_ref.shape[-1]
    for il, ref in enumerate((a_ref, b_ref)):
        for core in range(2):
            hi, lo = halves(ref[core])
            o_ref[0, 2 * core + il, :, :w] = hi
            o_ref[0, 2 * core + il, :, w : 2 * w] = lo
            o_ref[0, 2 * core + il, :, 2 * w :] = hi


def split_amp(c, a):
    w = a.shape[-1]
    tile = lambda il: pl.BlockSpec((2, w, w), lambda g, m: (g, 2 * il + m[0], 0))
    return pl.pallas_call(
        split_kernel,
        grid_spec=pltpu.PrefetchScalarGridSpec(
            num_scalar_prefetch=1,
            grid=(4,),
            in_specs=[tile(0), tile(1)],
            out_specs=pl.BlockSpec((1, 4, w, 3 * w), lambda g, m: (g, 0, 0, 0)),
        ),
        out_shape=jax.ShapeDtypeStruct((4, 4, w, 3 * w), jnp.bfloat16),
        compiler_params=pltpu.CompilerParams(vmem_limit_bytes=12 * MIB),
        cost_estimate=pl.CostEstimate(flops=0, bytes_accessed=10 * MIB, transcendentals=0),
        name="split_amp",
    )(c, a, a)


def make_contract_kernel(kp, split):
    def kernel(flag_ref, a_ref, own, own_r, own_l, rest, two_r, two_l, own_fa, own_fb, fa, fb, *refs):
        outs, b_ref = refs[:-1], refs[-1]
        w = b_ref.shape[2]
        h = w // 2

        def load(s, b, at=0):
            n = b.shape[0]
            hi, lo = halves(b)
            b_ref[s, at : at + n] = hi
            b_ref[s, w + at : w + at + n] = hi
            b_ref[s, 2 * w + at : 2 * w + at + n] = lo

        z, c, x = flag_ref[128], flag_ref[129], flag_ref[130]

        @pl.loop(0, 4)
        def _(step):
            ka = lax.rem(z + jnp.where(step == 1, 3, jnp.where(step == 2, 1, jnp.where(step == 3, 2, 0))), 4)
            for at, (mine, others) in enumerate(((own, rest), (own_r, two_r), (own_l, two_l))):
                @pl.when(step == at)
                def _():
                    load(0, mine[kp])
                    for s in range(3):
                        load(s + 1, others[s])

            @pl.when(step == 3)
            def _():
                for part, (mine, others) in enumerate(((own_fa, fa), (own_fb, fb))):
                    load(0, mine[3, kp * h : kp * h + h], part * h)
                    for s in range(3):
                        load(s + 1, others[s], part * h)

            for turn in range(2):
                core = lax.rem(c + turn, 2) if split else turn
                for il in range(2):
                    out, at = (outs[turn], (ka, il)) if split else (outs[0], (ka, 2 * turn + il))
                    out[at] = jnp.zeros((w, w), jnp.float32)
                    for s in range(4):
                        jx = lax.rem(x + s, 4)

                        @pl.when(flag_ref[(jx * 2 + core) * 16 + kp * 8 + ka * 2 + il] != 0)
                        def _():
                            out[at] += jnp.dot(
                                a_ref[jx, 2 * core + il], b_ref[s], preferred_element_type=jnp.float32
                            )

    return kernel


def contract(kp, split, flags, a3, pieces):
    w = a3.shape[2]
    inside = pl.BlockSpec(memory_space=pltpu.VMEM)
    out = [jax.ShapeDtypeStruct((4, 2, w, w), jnp.float32)] * 2 if split else [
        jax.ShapeDtypeStruct((4, 4, w, w), jnp.float32)]
    return pl.pallas_call(
        make_contract_kernel(kp, split),
        in_specs=[pl.BlockSpec(memory_space=pltpu.SMEM)] + [inside] * (len(pieces) + 1),
        out_specs=[inside] * len(out),
        scratch_shapes=[pltpu.VMEM((4, 3 * w, w), jnp.bfloat16)],
        out_shape=out,
        compiler_params=pltpu.CompilerParams(vmem_limit_bytes=28 * MIB),
        cost_estimate=pl.CostEstimate(flops=40 * 10**9, bytes_accessed=8 * MIB, transcendentals=0),
        name="contract",
    )(flags, a3, *pieces)


def on_device(amp, integ, resid, triples):
    w = amp.shape[-1]
    h = w // 2
    z, c, y, x = (lax.axis_index(n) for n in NAMES)

    tri = triples[0, 0]
    i = tri[0] // 32
    j = tri[0] % 32
    k = tri[1] % 32
    slot = (((j % 2 * 4 + (k // 2) % 4) * 2 + k % 2) * 4 + k // 8) * 2 + i % 2
    place = lax.broadcasted_iota(jnp.int32, (32, w), 1)
    listed = jnp.sum((place == slot[:, None]).astype(jnp.float32), axis=0, keepdims=True)

    gathered = lax.all_gather(
        jnp.concatenate([amp.reshape(4 * w, w), jnp.broadcast_to(listed, (8, w))]), ("x", "c")
    )
    a3 = split_amp(c[None], gathered)
    flags = lax.dynamic_index_in_dim(gathered[:, 4 * w, :128].reshape(4, 2, 8, 16), c * 4 + x, 2, keepdims=False)
    flags = jnp.concatenate([flags.reshape(-1).astype(jnp.int32), jnp.stack([z, c, x])])

    mine = lax.dynamic_index_in_dim(integ, c, 0, keepdims=False)
    other = shift(lax.dynamic_index_in_dim(integ, 1 - c, 0, keepdims=False), "c", 1)
    pairs = jnp.where(c == 0, jnp.stack([mine, other]), jnp.stack([other, mine])).reshape(4, 2, w, w)
    own = lax.dynamic_index_in_dim(pairs, x, 0, keepdims=False)
    own_r, own_l = shift(own, "z", 1), shift(own, "z", -1)

    def others(kp):
        held = lax.all_to_all(pairs[:, kp], "x", 0, 0, tiled=True)
        return lax.dynamic_slice_in_dim(jnp.concatenate([held, held]), x + 1, 3, 0)

    rest = [others(0), others(1)]

    two_r = shift(jnp.concatenate([rest[0], own_r[:, :h].reshape(1, w, w)]), "z", 1)
    two_l = shift(jnp.concatenate([rest[0], own_l[:, h:].reshape(1, w, w)]), "z", -1)
    two_r, two_l, rest[1] = lax.optimization_barrier((two_r, two_l, rest[1]))
    far0 = shift(two_r[:3, :h], "z", 1), shift(two_l[:3, h:], "z", -1)
    rest1_r, rest1_l = shift(rest[1], "z", 1), shift(rest[1], "z", -1)
    far1 = shift(rest1_r[:, :h], "z", 1), shift(rest1_l[:, h:], "z", -1)

    pieces = own, own_r, own_l
    (part,) = contract(0, False, flags, a3, pieces + (rest[0], two_r, two_l, two_r, two_l) + far0)
    even = lax.psum_scatter(part.reshape(16, w, w), ("y", "c"), scatter_dimension=0, tiled=True)
    held, away = contract(1, True, flags, a3, pieces + (rest[1], rest1_r, rest1_l, two_r, two_l) + far1)
    part = lax.all_to_all(held + shift(away, "c", 1), "y", 0, 0, tiled=True)
    return resid + jnp.stack([even, part[0] + part[1] + part[2] + part[3]], axis=1)


def solution(mesh):
    fine = Mesh(mesh.devices.reshape(4, 2, 4, 4), NAMES)
    row, col = ("z", "c"), ("y", "x")
    return jax.shard_map(
        on_device,
        mesh=fine,
        in_specs=(P(row, col), P(col, row), P(row, col), P(row, col)),
        out_specs=P(row, col),
        check_vma=False,
    )
```

```python
import jax
import jax.numpy as jnp
from jax import lax
from jax.experimental import pallas as pl
from jax.experimental.pallas import tpu as pltpu
from jax.sharding import Mesh, PartitionSpec as P

NAMES = ("z", "c", "y", "x")
SIZE = {"z": 4, "c": 2, "y": 4, "x": 4}
MIB = 1024 * 1024
COST = (40, 40)

def shift(t, axis, s):
    n = SIZE[axis]
    return lax.ppermute(t, axis, [(i, (i + s) % n) for i in range(n)])


def halves(a):
    hi = a.astype(jnp.bfloat16)
    return hi, (a - hi.astype(jnp.float32)).astype(jnp.bfloat16)


def split_kernel(a_ref, r_ref, l_ref, fa_ref, fb_ref, o_ref):
    w = a_ref.shape[-1]

    def put(s, ref):
        for il in range(2):
            hi, lo = halves(ref[0, il * w : il * w + w])
            o_ref[s, il, :, :w] = hi
            o_ref[s, il, :, w : 2 * w] = lo
            o_ref[s, il, :, 2 * w :] = hi

    put(0, a_ref)
    put(1, r_ref)
    put(3, l_ref)

    @pl.when(pl.program_id(0) == 0)
    def _():
        put(2, fa_ref)

    @pl.when(pl.program_id(0) == 1)
    def _():
        put(2, fb_ref)


def split_amp(a, r, l, fa, fb):
    rows, w = a.shape[1:]
    each = pl.BlockSpec((1, rows, w), lambda g: (g, 0, 0))
    only = pl.BlockSpec((1, rows, w), lambda g: (0, 0, 0))
    return pl.pallas_call(
        split_kernel,
        grid=(2,),
        in_specs=[each, each, each, only, only],
        out_specs=pl.BlockSpec((4, 2, w, 3 * w), lambda g: (0, g, 0, 0)),
        out_shape=jax.ShapeDtypeStruct((4, 4, w, 3 * w), jnp.bfloat16),
        compiler_params=pltpu.CompilerParams(vmem_limit_bytes=18 * MIB),
        cost_estimate=pl.CostEstimate(flops=0, bytes_accessed=10 * MIB, transcendentals=0),
        name="split_amp",
    )(a, r, l, fa, fb)


def make_contract_kernel(kp):
    def kernel(flag_ref, a_ref, own, own_r, own_l, rest, two_r, two_l, own_fa, own_fb, fa, fb, *refs):
        outs, b_ref = refs[:-1], refs[-1]
        w = b_ref.shape[2]
        h = w // 2

        def load(s, b, at=0):
            n = b.shape[0]
            hi, lo = halves(b)
            b_ref[s, at : at + n] = hi
            b_ref[s, w + at : w + at + n] = hi
            b_ref[s, 2 * w + at : 2 * w + at + n] = lo

        z, c = flag_ref[128], flag_ref[129]

        @pl.loop(0, 4)
        def _(step):
            ka = lax.rem(z + jnp.where(step == 1, 3, jnp.where(step == 2, 1, jnp.where(step == 3, 2, 0))), 4)
            for at, (mine, others) in enumerate(((own, rest), (own_r, two_r), (own_l, two_l))):
                @pl.when(step == at)
                def _():
                    load(0, mine[kp])
                    for s in range(3):
                        load(s + 1, others[s])

            @pl.when(step == 3)
            def _():
                for part, (mine, others) in enumerate(((own_fa, fa), (own_fb, fb))):
                    load(0, mine[3, kp * h : kp * h + h], part * h)
                    for s in range(3):
                        load(s + 1, others[s], part * h)

            for turn in range(2):
                core = lax.rem(c + turn, 2)
                for il in range(2):
                    out, at = outs[turn], (ka, il)
                    out[at] = jnp.zeros((w, w), jnp.float32)
                    for s in range(4):
                        @pl.when(flag_ref[(s * 2 + core) * 16 + kp * 8 + ka * 2 + il] != 0)
                        def _():
                            out[at] += jnp.dot(
                                a_ref[s, 2 * core + il], b_ref[s], preferred_element_type=jnp.float32
                            )

    return kernel


def contract(kp, flags, a3, pieces):
    w = a3.shape[2]
    inside = pl.BlockSpec(memory_space=pltpu.VMEM)
    out = [jax.ShapeDtypeStruct((4, 2, w, w), jnp.float32)] * 2
    return pl.pallas_call(
        make_contract_kernel(kp),
        in_specs=[pl.BlockSpec(memory_space=pltpu.SMEM)] + [inside] * (len(pieces) + 1),
        out_specs=[inside] * len(out),
        scratch_shapes=[pltpu.VMEM((4, 3 * w, w), jnp.bfloat16)],
        out_shape=out,
        compiler_params=pltpu.CompilerParams(vmem_limit_bytes=28 * MIB),
        cost_estimate=pl.CostEstimate(flops=COST[kp] * 10**9, bytes_accessed=8 * MIB, transcendentals=0),
        name="contract",
    )(flags, a3, *pieces)


def on_device(amp, integ, resid, triples):
    w = amp.shape[-1]
    h = w // 2
    z, c, y, x = (lax.axis_index(n) for n in NAMES)

    tri = triples[0, 0]
    i = tri[0] // 32
    j = tri[0] % 32
    k = tri[1] % 32
    slot = (((j % 2 * 4 + (k // 2) % 4) * 2 + k % 2) * 4 + k // 8) * 2 + i % 2
    place = lax.broadcasted_iota(jnp.int32, (32, w), 1)
    listed = jnp.sum((place == slot[:, None]).astype(jnp.float32), axis=0, keepdims=True)

    mine = lax.dynamic_index_in_dim(integ, c, 0, keepdims=False)
    other = shift(lax.dynamic_index_in_dim(integ, 1 - c, 0, keepdims=False), "c", 1)
    pairs = jnp.where(c == 0, jnp.stack([mine, other]), jnp.stack([other, mine])).reshape(4, 2, w, w)
    own = lax.dynamic_index_in_dim(pairs, x, 0, keepdims=False)
    own_r, own_l = shift(own, "z", 1), shift(own, "z", -1)

    def others(kp):
        held = lax.all_to_all(pairs[:, kp], "x", 0, 0, tiled=True)
        return lax.dynamic_slice_in_dim(jnp.concatenate([held, held]), x + 1, 3, 0)

    rest = [others(0), others(1)]

    def with_flags(parity):
        tile = lax.dynamic_index_in_dim(amp, parity, 1, keepdims=False)
        return jnp.concatenate([tile.reshape(2 * w, w), jnp.broadcast_to(listed, (8, w))])

    a_mine, a_other = with_flags(c), shift(with_flags(1 - c), "c", 1)
    a0 = jnp.where(c == 0, jnp.stack([a_mine, a_other]), jnp.stack([a_other, a_mine]))
    a0, rest[0] = lax.optimization_barrier((a0, rest[0]))
    a_r, a_l = shift(a0, "x", -1), shift(a0, "x", 1)
    a_fa, a_fb = shift(a_r[:1], "x", -1), shift(a_l[1:], "x", 1)
    a3 = split_amp(a0, a_r, a_l, a_fa, a_fb)
    rows = jnp.stack([a0[:, 2 * w, :128], a_r[:, 2 * w, :128],
                      jnp.concatenate([a_fa[:, 2 * w, :128], a_fb[:, 2 * w, :128]]), a_l[:, 2 * w, :128]])
    flags = lax.dynamic_index_in_dim(rows.reshape(4, 2, 8, 16), c * 4 + x, 2, keepdims=False)
    flags = jnp.concatenate([flags.reshape(-1).astype(jnp.int32), jnp.stack([z, c])])

    two_r = shift(jnp.concatenate([rest[0], own_r[:, :h].reshape(1, w, w)]), "z", 1)
    two_l = shift(jnp.concatenate([rest[0], own_l[:, h:].reshape(1, w, w)]), "z", -1)
    two_r, two_l, rest[1] = lax.optimization_barrier((two_r, two_l, rest[1]))
    far0 = shift(two_r[:3, :h], "z", 1), shift(two_l[:3, h:], "z", -1)
    rest1_r, rest1_l = shift(rest[1], "z", 1), shift(rest[1], "z", -1)
    a3, rest1_r, rest1_l = lax.optimization_barrier((a3, rest1_r, rest1_l))
    far1 = shift(rest1_r[:, :h], "z", 1), shift(rest1_l[:, h:], "z", -1)

    pieces = own, own_r, own_l
    held, away = contract(0, flags, a3, pieces + (rest[0], two_r, two_l, two_r, two_l) + far0)
    part = held + shift(away, "c", 1)
    part = lax.all_to_all(part, "y", 0, 0, tiled=True)
    gate = part
    even = part[0] + part[1] + part[2] + part[3]
    held, away = contract(1, flags, a3, pieces + (rest[1], rest1_r, rest1_l, two_r, two_l) + far1)
    away, gate = lax.optimization_barrier((away, gate))
    part = lax.all_to_all(held + shift(away, "c", 1), "y", 0, 0, tiled=True)
    return resid + jnp.stack([even, part[0] + part[1] + part[2] + part[3]], axis=1)


def solution(mesh):
    fine = Mesh(mesh.devices.reshape(4, 2, 4, 4), NAMES)
    row, col = ("z", "c"), ("y", "x")
    return jax.shard_map(
        on_device,
        mesh=fine,
        in_specs=(P(row, col), P(col, row), P(row, col), P(row, col)),
        out_specs=P(row, col),
        check_vma=False,
    )
```

```python
import jax
import jax.numpy as jnp
from jax import lax
from jax.experimental import pallas as pl
from jax.experimental.pallas import tpu as pltpu
from jax.sharding import Mesh, PartitionSpec as P

NAMES = ("z", "c", "y", "x")
SIZE = {"z": 4, "c": 2, "y": 4, "x": 4}
MIB = 1024 * 1024
COST = (40, 40)

def shift(t, axis, s):
    n = SIZE[axis]
    return lax.ppermute(t, axis, [(i, (i + s) % n) for i in range(n)])


def halves(a):
    hi = a.astype(jnp.bfloat16)
    return hi, (a - hi.astype(jnp.float32)).astype(jnp.bfloat16)


def split_kernel(a_ref, r_ref, l_ref, fa_ref, fb_ref, o_ref):
    w = a_ref.shape[-1]

    def put(s, ref):
        for il in range(2):
            hi, lo = halves(ref[0, il * w : il * w + w])
            o_ref[s, il, :, :w] = hi
            o_ref[s, il, :, w : 2 * w] = lo
            o_ref[s, il, :, 2 * w :] = hi

    put(0, a_ref)
    put(1, r_ref)
    put(3, l_ref)

    @pl.when(pl.program_id(0) == 0)
    def _():
        put(2, fa_ref)

    @pl.when(pl.program_id(0) == 1)
    def _():
        put(2, fb_ref)


def split_amp(a, r, l, fa, fb):
    rows, w = a.shape[1:]
    each = pl.BlockSpec((1, rows, w), lambda g: (g, 0, 0))
    only = pl.BlockSpec((1, rows, w), lambda g: (0, 0, 0))
    return pl.pallas_call(
        split_kernel,
        grid=(2,),
        in_specs=[each, each, each, only, only],
        out_specs=pl.BlockSpec((4, 2, w, 3 * w), lambda g: (0, g, 0, 0)),
        out_shape=jax.ShapeDtypeStruct((4, 4, w, 3 * w), jnp.bfloat16),
        compiler_params=pltpu.CompilerParams(vmem_limit_bytes=18 * MIB),
        cost_estimate=pl.CostEstimate(flops=0, bytes_accessed=10 * MIB, transcendentals=0),
        name="split_amp",
    )(a, r, l, fa, fb)


def make_contract_kernel(kp):
    def kernel(flag_ref, a_ref, own, own_r, own_l, rest, two_r, two_l, own_fa, own_fb, fa, fb, *refs):
        outs, b_ref = refs[:-1], refs[-1]
        w = b_ref.shape[2]
        h = w // 2

        def load(s, b, at=0):
            n = b.shape[0]
            hi, lo = halves(b)
            b_ref[s, at : at + n] = hi
            b_ref[s, w + at : w + at + n] = hi
            b_ref[s, 2 * w + at : 2 * w + at + n] = lo

        z, c = flag_ref[128], flag_ref[129]

        @pl.loop(0, 4)
        def _(step):
            ka = lax.rem(z + jnp.where(step == 1, 3, jnp.where(step == 2, 1, jnp.where(step == 3, 2, 0))), 4)
            for at, (mine, others) in enumerate(((own, rest), (own_r, two_r), (own_l, two_l))):
                @pl.when(step == at)
                def _():
                    load(0, mine[kp])
                    for s in range(3):
                        load(s + 1, others[s])

            @pl.when(step == 3)
            def _():
                for part, (mine, others) in enumerate(((own_fa, fa), (own_fb, fb))):
                    load(0, mine[3, kp * h : kp * h + h], part * h)
                    for s in range(3):
                        load(s + 1, others[s], part * h)

            for turn in range(2):
                core = lax.rem(c + turn, 2)
                for il in range(2):
                    out, at = outs[turn], (ka, il)
                    out[at] = jnp.zeros((w, w), jnp.float32)
                    for s in range(4):
                        @pl.when(flag_ref[(s * 2 + core) * 16 + kp * 8 + ka * 2 + il] != 0)
                        def _():
                            out[at] += jnp.dot(
                                a_ref[s, 2 * core + il], b_ref[s], preferred_element_type=jnp.float32
                            )

    return kernel


def contract(kp, flags, a3, pieces):
    w = a3.shape[2]
    inside = pl.BlockSpec(memory_space=pltpu.VMEM)
    out = [jax.ShapeDtypeStruct((4, 2, w, w), jnp.float32)] * 2
    return pl.pallas_call(
        make_contract_kernel(kp),
        in_specs=[pl.BlockSpec(memory_space=pltpu.SMEM)] + [inside] * (len(pieces) + 1),
        out_specs=[inside] * len(out),
        scratch_shapes=[pltpu.VMEM((4, 3 * w, w), jnp.bfloat16)],
        out_shape=out,
        compiler_params=pltpu.CompilerParams(vmem_limit_bytes=28 * MIB),
        cost_estimate=pl.CostEstimate(flops=COST[kp] * 10**9, bytes_accessed=8 * MIB, transcendentals=0),
        name="contract",
    )(flags, a3, *pieces)


def on_device(amp, integ, resid, triples):
    w = amp.shape[-1]
    h = w // 2
    z, c, y, x = (lax.axis_index(n) for n in NAMES)

    tri = triples[0, 0]
    i = tri[0] // 32
    j = tri[0] % 32
    k = tri[1] % 32
    slot = (((j % 2 * 4 + (k // 2) % 4) * 2 + k % 2) * 4 + k // 8) * 2 + i % 2
    place = lax.broadcasted_iota(jnp.int32, (32, w), 1)
    listed = jnp.sum((place == slot[:, None]).astype(jnp.float32), axis=0, keepdims=True)

    mine = lax.dynamic_index_in_dim(integ, c, 0, keepdims=False)
    other = shift(lax.dynamic_index_in_dim(integ, 1 - c, 0, keepdims=False), "c", 1)
    pairs = jnp.where(c == 0, jnp.stack([mine, other]), jnp.stack([other, mine])).reshape(4, 2, w, w)
    own = lax.dynamic_index_in_dim(pairs, x, 0, keepdims=False)
    own, pairs = lax.optimization_barrier((own, pairs))
    own_r, own_l = shift(own, "z", 1), shift(own, "z", -1)

    came = [
        shift(lax.dynamic_slice(pairs, (lax.rem(x + 4 - s, 4), 0, 0, 0), (1, 1, w, w)).reshape(w, w), "x", -s)
        for s in (1, 2, 3)
    ]
    rest = [jnp.stack(came)]
    pairs, rest[0], own_r, own_l = lax.optimization_barrier((pairs, rest[0], own_r, own_l))
    held = lax.all_to_all(pairs[:, 1], "x", 0, 0, tiled=True)
    rest.append(lax.dynamic_slice_in_dim(jnp.concatenate([held, held]), x + 1, 3, 0))

    def with_flags(parity):
        tile = lax.dynamic_index_in_dim(amp, parity, 1, keepdims=False)
        return jnp.concatenate([tile.reshape(2 * w, w), jnp.broadcast_to(listed, (8, w))])

    a_mine, a_other = with_flags(c), shift(with_flags(1 - c), "c", 1)
    a0 = jnp.where(c == 0, jnp.stack([a_mine, a_other]), jnp.stack([a_other, a_mine]))
    a0, rest[1] = lax.optimization_barrier((a0, rest[1]))
    a_r, a_l = shift(a0, "x", -1), shift(a0, "x", 1)
    a_fa, a_fb = shift(a_r[:1], "x", -1), shift(a_l[1:], "x", 1)
    a3 = split_amp(a0, a_r, a_l, a_fa, a_fb)
    rows = jnp.stack([a0[:, 2 * w, :128], a_r[:, 2 * w, :128],
                      jnp.concatenate([a_fa[:, 2 * w, :128], a_fb[:, 2 * w, :128]]), a_l[:, 2 * w, :128]])
    flags = lax.dynamic_index_in_dim(rows.reshape(4, 2, 8, 16), c * 4 + x, 2, keepdims=False)
    flags = jnp.concatenate([flags.reshape(-1).astype(jnp.int32), jnp.stack([z, c])])

    two_r = shift(jnp.concatenate([rest[0], own_r[:, :h].reshape(1, w, w)]), "z", 1)
    two_l = shift(jnp.concatenate([rest[0], own_l[:, h:].reshape(1, w, w)]), "z", -1)
    two_r, two_l, rest[1] = lax.optimization_barrier((two_r, two_l, rest[1]))
    far0 = shift(two_r[:3, :h], "z", 1), shift(two_l[:3, h:], "z", -1)
    rest1_r, rest1_l = shift(rest[1], "z", 1), shift(rest[1], "z", -1)
    a3, rest1_r, rest1_l = lax.optimization_barrier((a3, rest1_r, rest1_l))
    far1 = shift(rest1_r[:, :h], "z", 1), shift(rest1_l[:, h:], "z", -1)

    pieces = own, own_r, own_l
    held, away = contract(0, flags, a3, pieces + (rest[0], two_r, two_l, two_r, two_l) + far0)
    part = held + shift(away, "c", 1)
    part = lax.all_to_all(part, "y", 0, 0, tiled=True)
    gate = part
    even = part[0] + part[1] + part[2] + part[3]
    held, away = contract(1, flags, a3, pieces + (rest[1], rest1_r, rest1_l, two_r, two_l) + far1)
    away, gate = lax.optimization_barrier((away, gate))
    part = lax.all_to_all(held + shift(away, "c", 1), "y", 0, 0, tiled=True)
    return resid + jnp.stack([even, part[0] + part[1] + part[2] + part[3]], axis=1)


def solution(mesh):
    fine = Mesh(mesh.devices.reshape(4, 2, 4, 4), NAMES)
    row, col = ("z", "c"), ("y", "x")
    return jax.shard_map(
        on_device,
        mesh=fine,
        in_specs=(P(row, col), P(col, row), P(row, col), P(row, col)),
        out_specs=P(row, col),
        check_vma=False,
    )
```

```python
import jax
import jax.numpy as jnp
from jax import lax
from jax.experimental import pallas as pl
from jax.experimental.pallas import tpu as pltpu
from jax.sharding import Mesh, PartitionSpec as P

NAMES = ("z", "c", "y", "x")
SIZE = {"z": 4, "c": 2, "y": 4, "x": 4}
MIB = 1024 * 1024
COST = (40, 40)

def shift(t, axis, s):
    n = SIZE[axis]
    return lax.ppermute(t, axis, [(i, (i + s) % n) for i in range(n)])


def halves(a):
    hi = a.astype(jnp.bfloat16)
    return hi, (a - hi.astype(jnp.float32)).astype(jnp.bfloat16)


def split_kernel(a_ref, r_ref, l_ref, fa_ref, fb_ref, o_ref):
    w = a_ref.shape[-1]

    def put(s, ref):
        for il in range(2):
            hi, lo = halves(ref[0, il * w : il * w + w])
            o_ref[s, il, :, :w] = hi
            o_ref[s, il, :, w : 2 * w] = lo
            o_ref[s, il, :, 2 * w :] = hi

    put(0, a_ref)
    put(1, r_ref)
    put(3, l_ref)

    @pl.when(pl.program_id(0) == 0)
    def _():
        put(2, fa_ref)

    @pl.when(pl.program_id(0) == 1)
    def _():
        put(2, fb_ref)


def split_amp(a, r, l, fa, fb):
    rows, w = a.shape[1:]
    each = pl.BlockSpec((1, rows, w), lambda g: (g, 0, 0))
    only = pl.BlockSpec((1, rows, w), lambda g: (0, 0, 0))
    return pl.pallas_call(
        split_kernel,
        grid=(2,),
        in_specs=[each, each, each, only, only],
        out_specs=pl.BlockSpec((4, 2, w, 3 * w), lambda g: (0, g, 0, 0)),
        out_shape=jax.ShapeDtypeStruct((4, 4, w, 3 * w), jnp.bfloat16),
        compiler_params=pltpu.CompilerParams(vmem_limit_bytes=18 * MIB),
        cost_estimate=pl.CostEstimate(flops=0, bytes_accessed=10 * MIB, transcendentals=0),
        name="split_amp",
    )(a, r, l, fa, fb)


def make_contract_kernel(kp):
    def kernel(flag_ref, amp_ref, own, own_r, own_l, rest, two_r, two_l, own_fa, own_fb, fa, fb,
               mine_ref, other_ref, a_ref, near_ref, far_ref, b_ref, sems):
        w = b_ref.shape[2]
        h = w // 2
        three = pl.ds(0, 3)
        pairs = []
        for step, (mine, others) in enumerate(((own, rest), (own_r, two_r), (own_l, two_l))):
            pairs.append((mine.at[kp], near_ref.at[step, 0]))
            pairs.append((others.at[three], near_ref.at[step, pl.ds(1, 3)]))
        for part, (mine, others) in enumerate(((own_fa, fa), (own_fb, fb))):
            rows = pl.ds(part * h, h)
            pairs.append((mine.at[3, pl.ds(kp * h, h)], far_ref.at[0, rows]))
            pairs.append((others.at[three], far_ref.at[pl.ds(1, 3), rows]))
        pairs.append((amp_ref, a_ref))
        copies = [pltpu.make_async_copy(*pair, sems.at[n]) for n, pair in enumerate(pairs)]
        for n in (0, 1, 10, 2, 3, 4, 5, 6, 7, 8, 9):
            copies[n].start()

        def load(ref):
            for s in range(4):
                hi, lo = halves(ref[s])
                b_ref[s, :w] = hi
                b_ref[s, w : 2 * w] = hi
                b_ref[s, 2 * w :] = lo

        z, c = flag_ref[128], flag_ref[129]

        @pl.loop(0, 4)
        def _(step):
            ka = lax.rem(z + jnp.where(step == 1, 3, jnp.where(step == 2, 1, jnp.where(step == 3, 2, 0))), 4)
            for at in range(3):
                @pl.when(step == at)
                def _():
                    copies[2 * at].wait()
                    copies[2 * at + 1].wait()
                    load(near_ref.at[at])

            @pl.when(step == 0)
            def _():
                copies[10].wait()

            @pl.when(step == 3)
            def _():
                for n in range(6, 10):
                    copies[n].wait()
                load(far_ref)

            for turn in range(2):
                core = lax.rem(c + turn, 2)
                for il in range(2):
                    out, at = (mine_ref, other_ref)[turn], (ka, il)
                    out[at] = jnp.zeros((w, w), jnp.float32)
                    for s in range(4):
                        @pl.when(flag_ref[(s * 2 + core) * 16 + kp * 8 + ka * 2 + il] != 0)
                        def _():
                            out[at] += jnp.dot(
                                a_ref[s, 2 * core + il], b_ref[s], preferred_element_type=jnp.float32
                            )

    return kernel


def contract(kp, flags, a3, pieces):
    w = a3.shape[2]
    inside = pl.BlockSpec(memory_space=pltpu.VMEM)
    anywhere = pl.BlockSpec(memory_space=pl.ANY)
    out = [jax.ShapeDtypeStruct((4, 2, w, w), jnp.float32)] * 2
    return pl.pallas_call(
        make_contract_kernel(kp),
        in_specs=[pl.BlockSpec(memory_space=pltpu.SMEM)] + [anywhere] * (len(pieces) + 1),
        out_specs=[inside] * 2,
        scratch_shapes=[
            pltpu.VMEM(a3.shape, jnp.bfloat16),
            pltpu.VMEM((3, 4, w, w), jnp.float32),
            pltpu.VMEM((4, w, w), jnp.float32),
            pltpu.VMEM((4, 3 * w, w), jnp.bfloat16),
            pltpu.SemaphoreType.DMA((11,)),
        ],
        out_shape=out,
        compiler_params=pltpu.CompilerParams(vmem_limit_bytes=28 * MIB),
        cost_estimate=pl.CostEstimate(flops=COST[kp] * 10**9, bytes_accessed=8 * MIB, transcendentals=0),
        name="contract",
    )(flags, a3, *pieces)


def on_device(amp, integ, resid, triples):
    w = amp.shape[-1]
    h = w // 2
    z, c, y, x = (lax.axis_index(n) for n in NAMES)

    tri = triples[0, 0]
    i = tri[0] // 32
    j = tri[0] % 32
    k = tri[1] % 32
    slot = (((j % 2 * 4 + (k // 2) % 4) * 2 + k % 2) * 4 + k // 8) * 2 + i % 2
    place = lax.broadcasted_iota(jnp.int32, (32, w), 1)
    listed = jnp.sum((place == slot[:, None]).astype(jnp.float32), axis=0, keepdims=True)

    mine = lax.dynamic_index_in_dim(integ, c, 0, keepdims=False)
    other = shift(lax.dynamic_index_in_dim(integ, 1 - c, 0, keepdims=False), "c", 1)
    pairs = jnp.where(c == 0, jnp.stack([mine, other]), jnp.stack([other, mine])).reshape(4, 2, w, w)
    own = lax.dynamic_index_in_dim(pairs, x, 0, keepdims=False)
    own, pairs = lax.optimization_barrier((own, pairs))
    own_r, own_l = shift(own, "z", 1), shift(own, "z", -1)

    came = [
        shift(lax.dynamic_slice(pairs, (lax.rem(x + 4 - s, 4), 0, 0, 0), (1, 1, w, w)).reshape(w, w), "x", -s)
        for s in (1, 2, 3)
    ]
    rest = [jnp.stack(came)]

    def with_flags(parity):
        tile = lax.dynamic_index_in_dim(amp, parity, 1, keepdims=False)
        return jnp.concatenate([tile.reshape(2 * w, w), jnp.broadcast_to(listed, (8, w))])

    a_mine, a_other = with_flags(c), shift(with_flags(1 - c), "c", 1)
    a0 = jnp.where(c == 0, jnp.stack([a_mine, a_other]), jnp.stack([a_other, a_mine]))
    send_r = jnp.concatenate([rest[0], own_r[:, :h].reshape(1, w, w)])
    send_l = jnp.concatenate([rest[0], own_l[:, h:].reshape(1, w, w)])
    pairs, a0, send_r, send_l = lax.optimization_barrier((pairs, a0, send_r, send_l))
    two_r, two_l = shift(send_r, "z", 1), shift(send_l, "z", -1)
    held = lax.all_to_all(pairs[:, 1], "x", 0, 0, tiled=True)
    rest.append(lax.dynamic_slice_in_dim(jnp.concatenate([held, held]), x + 1, 3, 0))
    a0, rest[1] = lax.optimization_barrier((a0, rest[1]))
    a_r, a_l = shift(a0, "x", -1), shift(a0, "x", 1)
    a_fa, a_fb = shift(a_r[:1], "x", -1), shift(a_l[1:], "x", 1)
    a3 = split_amp(a0, a_r, a_l, a_fa, a_fb)
    rows = jnp.stack([a0[:, 2 * w, :128], a_r[:, 2 * w, :128],
                      jnp.concatenate([a_fa[:, 2 * w, :128], a_fb[:, 2 * w, :128]]), a_l[:, 2 * w, :128]])
    flags = lax.dynamic_index_in_dim(rows.reshape(4, 2, 8, 16), c * 4 + x, 2, keepdims=False)
    flags = jnp.concatenate([flags.reshape(-1).astype(jnp.int32), jnp.stack([z, c])])

    two_r, two_l, rest[1] = lax.optimization_barrier((two_r, two_l, rest[1]))
    far0 = shift(two_r[:3, :h], "z", 1), shift(two_l[:3, h:], "z", -1)
    rest1_r, rest1_l = shift(rest[1], "z", 1), shift(rest[1], "z", -1)
    a3, rest1_r, rest1_l = lax.optimization_barrier((a3, rest1_r, rest1_l))
    far1 = shift(rest1_r[:, :h], "z", 1), shift(rest1_l[:, h:], "z", -1)

    pieces = own, own_r, own_l
    held, away = contract(0, flags, a3, pieces + (rest[0], two_r, two_l, two_r, two_l) + far0)
    part = held + shift(away, "c", 1)
    part = lax.all_to_all(part, "y", 0, 0, tiled=True)
    gate = part
    even = part[0] + part[1] + part[2] + part[3]
    held, away = contract(1, flags, a3, pieces + (rest[1], rest1_r, rest1_l, two_r, two_l) + far1)
    away, gate = lax.optimization_barrier((away, gate))
    part = lax.all_to_all(held + shift(away, "c", 1), "y", 0, 0, tiled=True)
    return resid + jnp.stack([even, part[0] + part[1] + part[2] + part[3]], axis=1)


def solution(mesh):
    fine = Mesh(mesh.devices.reshape(4, 2, 4, 4), NAMES)
    row, col = ("z", "c"), ("y", "x")
    return jax.shard_map(
        on_device,
        mesh=fine,
        in_specs=(P(row, col), P(col, row), P(row, col), P(row, col)),
        out_specs=P(row, col),
        check_vma=False,
    )
```

```python
import jax
import jax.numpy as jnp
from jax import lax
from jax.experimental import pallas as pl
from jax.experimental.pallas import tpu as pltpu
from jax.sharding import Mesh, PartitionSpec as P

NAMES = ("z", "c", "y", "x")
SIZE = {"z": 4, "c": 2, "y": 4, "x": 4}
MIB = 1024 * 1024
COST = (50, 50)

def shift(t, axis, s):
    n = SIZE[axis]
    return lax.ppermute(t, axis, [(i, (i + s) % n) for i in range(n)])


def halves(a):
    hi = a.astype(jnp.bfloat16)
    return hi, (a - hi.astype(jnp.float32)).astype(jnp.bfloat16)


def split_kernel(c_ref, a_ref, b_ref, o_ref):
    w = a_ref.shape[-1]
    for il, ref in enumerate((a_ref, b_ref)):
        for core in range(2):
            hi, lo = halves(ref[core])
            o_ref[0, 2 * core + il, :, :w] = hi
            o_ref[0, 2 * core + il, :, w : 2 * w] = lo
            o_ref[0, 2 * core + il, :, 2 * w :] = hi


def split_amp(c, a):
    w = a.shape[-1]
    tile = lambda il: pl.BlockSpec((2, w, w), lambda g, m: (g, 2 * il + m[0], 0))
    return pl.pallas_call(
        split_kernel,
        grid_spec=pltpu.PrefetchScalarGridSpec(
            num_scalar_prefetch=1,
            grid=(4,),
            in_specs=[tile(0), tile(1)],
            out_specs=pl.BlockSpec((1, 4, w, 3 * w), lambda g, m: (g, 0, 0, 0)),
        ),
        out_shape=jax.ShapeDtypeStruct((4, 4, w, 3 * w), jnp.bfloat16),
        compiler_params=pltpu.CompilerParams(vmem_limit_bytes=12 * MIB),
        cost_estimate=pl.CostEstimate(flops=0, bytes_accessed=10 * MIB, transcendentals=0),
        name="split_amp",
    )(c, a, a)


def make_contract_kernel(kp, split):
    def kernel(flag_ref, a_ref, own, own_r, own_l, rest, two_r, two_l, own_fa, own_fb, fa, fb, *refs):
        outs, b_ref = refs[:-1], refs[-1]
        w = b_ref.shape[2]
        h = w // 2

        def load(s, b, at=0):
            n = b.shape[0]
            hi, lo = halves(b)
            b_ref[s, at : at + n] = hi
            b_ref[s, w + at : w + at + n] = hi
            b_ref[s, 2 * w + at : 2 * w + at + n] = lo

        z, c, x = flag_ref[128], flag_ref[129], flag_ref[130]

        @pl.loop(0, 4)
        def _(step):
            ka = lax.rem(z + jnp.where(step == 1, 3, jnp.where(step == 2, 1, jnp.where(step == 3, 2, 0))), 4)
            for at, (mine, others) in enumerate(((own, rest), (own_r, two_r), (own_l, two_l))):
                @pl.when(step == at)
                def _():
                    load(0, mine[kp])
                    for s in range(3):
                        load(s + 1, others[s])

            @pl.when(step == 3)
            def _():
                for part, (mine, others) in enumerate(((own_fa, fa), (own_fb, fb))):
                    load(0, mine[3, kp * h : kp * h + h], part * h)
                    for s in range(3):
                        load(s + 1, others[s], part * h)

            for turn in range(2):
                core = lax.rem(c + turn, 2) if split else turn
                for il in range(2):
                    out, at = (outs[turn], (ka, il)) if split else (outs[0], (ka, 2 * turn + il))
                    out[at] = jnp.zeros((w, w), jnp.float32)
                    for s in range(4):
                        jx = lax.rem(x + s, 4)

                        @pl.when(flag_ref[(jx * 2 + core) * 16 + kp * 8 + ka * 2 + il] != 0)
                        def _():
                            out[at] += jnp.dot(
                                a_ref[jx, 2 * core + il], b_ref[s], preferred_element_type=jnp.float32
                            )

    return kernel


def contract(kp, split, flags, a3, pieces):
    w = a3.shape[2]
    inside = pl.BlockSpec(memory_space=pltpu.VMEM)
    out = [jax.ShapeDtypeStruct((4, 2, w, w), jnp.float32)] * 2 if split else [
        jax.ShapeDtypeStruct((4, 4, w, w), jnp.float32)]
    return pl.pallas_call(
        make_contract_kernel(kp, split),
        in_specs=[pl.BlockSpec(memory_space=pltpu.SMEM)] + [inside] * (len(pieces) + 1),
        out_specs=[inside] * len(out),
        scratch_shapes=[pltpu.VMEM((4, 3 * w, w), jnp.bfloat16)],
        out_shape=out,
        compiler_params=pltpu.CompilerParams(vmem_limit_bytes=28 * MIB),
        cost_estimate=pl.CostEstimate(flops=COST[kp] * 10**9, bytes_accessed=8 * MIB, transcendentals=0),
        name="contract",
    )(flags, a3, *pieces)


def on_device(amp, integ, resid, triples):
    w = amp.shape[-1]
    h = w // 2
    z, c, y, x = (lax.axis_index(n) for n in NAMES)

    tri = triples[0, 0]
    i = tri[0] // 32
    j = tri[0] % 32
    k = tri[1] % 32
    slot = (((j % 2 * 4 + (k // 2) % 4) * 2 + k % 2) * 4 + k // 8) * 2 + i % 2
    place = lax.broadcasted_iota(jnp.int32, (32, w), 1)
    listed = jnp.sum((place == slot[:, None]).astype(jnp.float32), axis=0, keepdims=True)

    gathered = lax.all_gather(
        jnp.concatenate([amp.reshape(4 * w, w), jnp.broadcast_to(listed, (8, w))]), ("x", "c")
    )
    a3 = split_amp(c[None], gathered)
    flags = lax.dynamic_index_in_dim(gathered[:, 4 * w, :128].reshape(4, 2, 8, 16), c * 4 + x, 2, keepdims=False)
    flags = jnp.concatenate([flags.reshape(-1).astype(jnp.int32), jnp.stack([z, c, x])])

    mine = lax.dynamic_index_in_dim(integ, c, 0, keepdims=False)
    other = shift(lax.dynamic_index_in_dim(integ, 1 - c, 0, keepdims=False), "c", 1)
    pairs = jnp.where(c == 0, jnp.stack([mine, other]), jnp.stack([other, mine])).reshape(4, 2, w, w)
    own = lax.dynamic_index_in_dim(pairs, x, 0, keepdims=False)
    own_r, own_l = shift(own, "z", 1), shift(own, "z", -1)

    def others(kp):
        held = lax.all_to_all(pairs[:, kp], "x", 0, 0, tiled=True)
        return lax.dynamic_slice_in_dim(jnp.concatenate([held, held]), x + 1, 3, 0)

    came = [
        shift(lax.dynamic_slice(pairs, (lax.rem(x + 4 - s, 4), 1, 0, 0), (1, 1, w, w)).reshape(w, w), "x", -s)
        for s in (1, 2, 3)
    ]
    rest = [others(0), jnp.stack(came)]

    two_r = shift(jnp.concatenate([rest[0], own_r[:, :h].reshape(1, w, w)]), "z", 1)
    two_l = shift(jnp.concatenate([rest[0], own_l[:, h:].reshape(1, w, w)]), "z", -1)
    two_r, two_l, rest[1] = lax.optimization_barrier((two_r, two_l, rest[1]))
    far0 = shift(two_r[:3, :h], "z", 1), shift(two_l[:3, h:], "z", -1)
    rest1_r, rest1_l = shift(rest[1], "z", 1), shift(rest[1], "z", -1)
    far1 = shift(rest1_r[:, :h], "z", 1), shift(rest1_l[:, h:], "z", -1)

    pieces = own, own_r, own_l
    (part,) = contract(0, False, flags, a3, pieces + (rest[0], two_r, two_l, two_r, two_l) + far0)
    even = lax.psum_scatter(part.reshape(16, w, w), ("y", "c"), scatter_dimension=0, tiled=True)
    held, away = contract(1, True, flags, a3, pieces + (rest[1], rest1_r, rest1_l, two_r, two_l) + far1)
    part = held + shift(away, "c", 1)
    part = [lax.dynamic_index_in_dim(part, lax.rem(y + s, 4), 0, keepdims=False) for s in range(4)]
    odd = part[0] + shift(part[1], "y", 1) + shift(part[2], "y", 2) + shift(part[3], "y", 3)
    return resid + jnp.stack([even, odd], axis=1)


def solution(mesh):
    fine = Mesh(mesh.devices.reshape(4, 2, 4, 4), NAMES)
    row, col = ("z", "c"), ("y", "x")
    return jax.shard_map(
        on_device,
        mesh=fine,
        in_specs=(P(row, col), P(col, row), P(row, col), P(row, col)),
        out_specs=P(row, col),
        check_vma=False,
    )
```

```python
import jax
import jax.numpy as jnp
from jax import lax
from jax.experimental import pallas as pl
from jax.experimental.pallas import tpu as pltpu
from jax.sharding import Mesh, PartitionSpec as P

NAMES = ("z", "c", "y", "x")
SIZE = {"z": 4, "c": 2, "y": 4, "x": 4}
MIB = 1024 * 1024
COST = (8, 8)

def shift(t, axis, s):
    n = SIZE[axis]
    return lax.ppermute(t, axis, [(i, (i + s) % n) for i in range(n)])


def halves(a):
    hi = a.astype(jnp.bfloat16)
    return hi, (a - hi.astype(jnp.float32)).astype(jnp.bfloat16)


def split_kernel(a_ref, r_ref, l_ref, fa_ref, fb_ref, o_ref):
    w = a_ref.shape[-1]

    def put(s, ref):
        for il in range(2):
            hi, lo = halves(ref[0, il * w : il * w + w])
            o_ref[s, il, :, :w] = hi
            o_ref[s, il, :, w : 2 * w] = lo
            o_ref[s, il, :, 2 * w :] = hi

    put(0, a_ref)
    put(1, r_ref)
    put(3, l_ref)

    @pl.when(pl.program_id(0) == 0)
    def _():
        put(2, fa_ref)

    @pl.when(pl.program_id(0) == 1)
    def _():
        put(2, fb_ref)


def split_amp(a, r, l, fa, fb):
    rows, w = a.shape[1:]
    each = pl.BlockSpec((1, rows, w), lambda g: (g, 0, 0))
    only = pl.BlockSpec((1, rows, w), lambda g: (0, 0, 0))
    return pl.pallas_call(
        split_kernel,
        grid=(2,),
        in_specs=[each, each, each, only, only],
        out_specs=pl.BlockSpec((4, 2, w, 3 * w), lambda g: (0, g, 0, 0)),
        out_shape=jax.ShapeDtypeStruct((4, 4, w, 3 * w), jnp.bfloat16),
        compiler_params=pltpu.CompilerParams(vmem_limit_bytes=18 * MIB),
        cost_estimate=pl.CostEstimate(flops=0, bytes_accessed=10 * MIB, transcendentals=0),
        name="split_amp",
    )(a, r, l, fa, fb)


def make_contract_kernel(kp):
    def kernel(flag_ref, a_ref, own, own_r, own_l, rest, two_r, two_l, own_fa, own_fb, fa, fb, *refs):
        outs, b_ref = refs[:-1], refs[-1]
        w = b_ref.shape[2]
        h = w // 2

        def load(s, b, at=0):
            n = b.shape[0]
            hi, lo = halves(b)
            b_ref[s, at : at + n] = hi
            b_ref[s, w + at : w + at + n] = hi
            b_ref[s, 2 * w + at : 2 * w + at + n] = lo

        z, c = flag_ref[128], flag_ref[129]

        @pl.loop(0, 4)
        def _(step):
            ka = lax.rem(z + jnp.where(step == 1, 3, jnp.where(step == 2, 1, jnp.where(step == 3, 2, 0))), 4)
            for at, (mine, others) in enumerate(((own, rest), (own_r, two_r), (own_l, two_l))):
                @pl.when(step == at)
                def _():
                    load(0, mine[kp])
                    for s in range(3):
                        load(s + 1, others[s])

            @pl.when(step == 3)
            def _():
                for part, (mine, others) in enumerate(((own_fa, fa), (own_fb, fb))):
                    load(0, mine[3, kp * h : kp * h + h], part * h)
                    for s in range(3):
                        load(s + 1, others[s], part * h)

            for turn in range(2):
                core = lax.rem(c + turn, 2)
                for il in range(2):
                    out, at = outs[turn], (ka, il)
                    out[at] = jnp.zeros((w, w), jnp.float32)
                    for s in range(4):
                        @pl.when(flag_ref[(s * 2 + core) * 16 + kp * 8 + ka * 2 + il] != 0)
                        def _():
                            out[at] += jnp.dot(
                                a_ref[s, 2 * core + il], b_ref[s], preferred_element_type=jnp.float32
                            )

    return kernel


def contract(kp, flags, a3, pieces):
    w = a3.shape[2]
    inside = pl.BlockSpec(memory_space=pltpu.VMEM)
    out = [jax.ShapeDtypeStruct((4, 2, w, w), jnp.float32)] * 2
    return pl.pallas_call(
        make_contract_kernel(kp),
        in_specs=[pl.BlockSpec(memory_space=pltpu.SMEM)] + [inside] * (len(pieces) + 1),
        out_specs=[inside] * len(out),
        scratch_shapes=[pltpu.VMEM((4, 3 * w, w), jnp.bfloat16)],
        out_shape=out,
        compiler_params=pltpu.CompilerParams(vmem_limit_bytes=28 * MIB),
        cost_estimate=pl.CostEstimate(flops=COST[kp] * 10**9, bytes_accessed=8 * MIB, transcendentals=0),
        name="contract",
    )(flags, a3, *pieces)


def on_device(amp, integ, resid, triples):
    w = amp.shape[-1]
    h = w // 2
    z, c, y, x = (lax.axis_index(n) for n in NAMES)

    tri = triples[0, 0]
    i = tri[0] // 32
    j = tri[0] % 32
    k = tri[1] % 32
    slot = (((j % 2 * 4 + (k // 2) % 4) * 2 + k % 2) * 4 + k // 8) * 2 + i % 2
    place = lax.broadcasted_iota(jnp.int32, (32, w), 1)
    listed = jnp.sum((place == slot[:, None]).astype(jnp.float32), axis=0, keepdims=True)

    mine = lax.dynamic_index_in_dim(integ, c, 0, keepdims=False)
    other = shift(lax.dynamic_index_in_dim(integ, 1 - c, 0, keepdims=False), "c", 1)
    pairs = jnp.where(c == 0, jnp.stack([mine, other]), jnp.stack([other, mine])).reshape(4, 2, w, w)
    own = lax.dynamic_index_in_dim(pairs, x, 0, keepdims=False)
    own, pairs = lax.optimization_barrier((own, pairs))
    own_r, own_l = shift(own, "z", 1), shift(own, "z", -1)

    came = [
        shift(lax.dynamic_index_in_dim(pairs, lax.rem(x + 4 - s, 4), 0, keepdims=False), "x", -s) for s in (1, 2, 3)
    ]
    rest = [jnp.stack([t[kp] for t in came]) for kp in range(2)]
    own_r, own_l, rest[0], rest[1] = lax.optimization_barrier((own_r, own_l, rest[0], rest[1]))

    def with_flags(parity):
        tile = lax.dynamic_index_in_dim(amp, parity, 1, keepdims=False)
        return jnp.concatenate([tile.reshape(2 * w, w), jnp.broadcast_to(listed, (8, w))])

    a_mine, a_other = with_flags(c), shift(with_flags(1 - c), "c", 1)
    a0 = jnp.where(c == 0, jnp.stack([a_mine, a_other]), jnp.stack([a_other, a_mine]))
    a0, rest[0] = lax.optimization_barrier((a0, rest[0]))
    a_r, a_l = shift(a0, "x", -1), shift(a0, "x", 1)
    a_fa, a_fb = shift(a_r[:1], "x", -1), shift(a_l[1:], "x", 1)
    a3 = split_amp(a0, a_r, a_l, a_fa, a_fb)
    rows = jnp.stack([a0[:, 2 * w, :128], a_r[:, 2 * w, :128],
                      jnp.concatenate([a_fa[:, 2 * w, :128], a_fb[:, 2 * w, :128]]), a_l[:, 2 * w, :128]])
    flags = lax.dynamic_index_in_dim(rows.reshape(4, 2, 8, 16), c * 4 + x, 2, keepdims=False)
    flags = jnp.concatenate([flags.reshape(-1).astype(jnp.int32), jnp.stack([z, c])])

    two_r = shift(jnp.concatenate([rest[0], own_r[:, :h].reshape(1, w, w)]), "z", 1)
    two_l = shift(jnp.concatenate([rest[0], own_l[:, h:].reshape(1, w, w)]), "z", -1)
    two_r, two_l, rest[1] = lax.optimization_barrier((two_r, two_l, rest[1]))
    far0 = shift(two_r[:3, :h], "z", 1), shift(two_l[:3, h:], "z", -1)
    rest1_r, rest1_l = shift(rest[1], "z", 1), shift(rest[1], "z", -1)
    far1 = shift(rest1_r[:, :h], "z", 1), shift(rest1_l[:, h:], "z", -1)

    pieces = own, own_r, own_l
    held, away = contract(0, flags, a3, pieces + (rest[0], two_r, two_l, two_r, two_l) + far0)
    part = held + shift(away, "c", 1)
    part = lax.all_to_all(part, "y", 0, 0, tiled=True)
    gate = part
    even = part[0] + part[1] + part[2] + part[3]
    held, away = contract(1, flags, a3, pieces + (rest[1], rest1_r, rest1_l, two_r, two_l) + far1)
    away, gate = lax.optimization_barrier((away, gate))
    part = lax.all_to_all(held + shift(away, "c", 1), "y", 0, 0, tiled=True)
    return resid + jnp.stack([even, part[0] + part[1] + part[2] + part[3]], axis=1)


def solution(mesh):
    fine = Mesh(mesh.devices.reshape(4, 2, 4, 4), NAMES)
    row, col = ("z", "c"), ("y", "x")
    return jax.shard_map(
        on_device,
        mesh=fine,
        in_specs=(P(row, col), P(col, row), P(row, col), P(row, col)),
        out_specs=P(row, col),
        check_vma=False,
    )
```

```python
import jax
import jax.numpy as jnp
from jax import lax
from jax.experimental import pallas as pl
from jax.experimental.pallas import tpu as pltpu
from jax.sharding import Mesh, PartitionSpec as P

NAMES = ("z", "c", "y", "x")
SIZE = {"z": 4, "c": 2, "y": 4, "x": 4}
MIB = 1024 * 1024
COST = (40, 40)

def shift(t, axis, s):
    n = SIZE[axis]
    return lax.ppermute(t, axis, [(i, (i + s) % n) for i in range(n)])


def halves(a):
    hi = a.astype(jnp.bfloat16)
    return hi, (a - hi.astype(jnp.float32)).astype(jnp.bfloat16)


def split_kernel(a_ref, r_ref, l_ref, fa_ref, fb_ref, o_ref):
    w = a_ref.shape[-1]

    def put(s, ref):
        for il in range(2):
            hi, lo = halves(ref[0, il * w : il * w + w])
            o_ref[s, il, :, :w] = hi
            o_ref[s, il, :, w : 2 * w] = lo
            o_ref[s, il, :, 2 * w :] = hi

    put(0, a_ref)
    put(1, r_ref)
    put(3, l_ref)

    @pl.when(pl.program_id(0) == 0)
    def _():
        put(2, fa_ref)

    @pl.when(pl.program_id(0) == 1)
    def _():
        put(2, fb_ref)


def split_amp(a, r, l, fa, fb):
    rows, w = a.shape[1:]
    each = pl.BlockSpec((1, rows, w), lambda g: (g, 0, 0))
    only = pl.BlockSpec((1, rows, w), lambda g: (0, 0, 0))
    return pl.pallas_call(
        split_kernel,
        grid=(2,),
        in_specs=[each, each, each, only, only],
        out_specs=pl.BlockSpec((4, 2, w, 3 * w), lambda g: (0, g, 0, 0)),
        out_shape=jax.ShapeDtypeStruct((4, 4, w, 3 * w), jnp.bfloat16),
        compiler_params=pltpu.CompilerParams(vmem_limit_bytes=18 * MIB),
        cost_estimate=pl.CostEstimate(flops=0, bytes_accessed=10 * MIB, transcendentals=0),
        name="split_amp",
    )(a, r, l, fa, fb)


def make_contract_kernel(kp):
    def kernel(flag_ref, a_ref, own, own_r, own_l, rest, two_r, two_l, own_fa, own_fb, fa, fb, *refs):
        outs, b_ref = refs[:-1], refs[-1]
        w = b_ref.shape[2]
        h = w // 2

        def load(s, b, at=0):
            n = b.shape[0]
            hi, lo = halves(b)
            b_ref[s, at : at + n] = hi
            b_ref[s, w + at : w + at + n] = hi
            b_ref[s, 2 * w + at : 2 * w + at + n] = lo

        z, c = flag_ref[128], flag_ref[129]

        @pl.loop(0, 4)
        def _(step):
            ka = lax.rem(z + jnp.where(step == 1, 3, jnp.where(step == 2, 1, jnp.where(step == 3, 2, 0))), 4)
            for at, (mine, others) in enumerate(((own, rest), (own_r, two_r), (own_l, two_l))):
                @pl.when(step == at)
                def _():
                    load(0, mine[kp])
                    for s in range(3):
                        load(s + 1, others[s])

            @pl.when(step == 3)
            def _():
                for part, (mine, others) in enumerate(((own_fa, fa), (own_fb, fb))):
                    load(0, mine[3, kp * h : kp * h + h], part * h)
                    for s in range(3):
                        load(s + 1, others[s], part * h)

            for turn in range(2):
                core = lax.rem(c + turn, 2)
                for il in range(2):
                    out, at = outs[turn], (ka, il)
                    out[at] = jnp.zeros((w, w), jnp.float32)
                    for s in range(4):
                        @pl.when(flag_ref[(s * 2 + core) * 16 + kp * 8 + ka * 2 + il] != 0)
                        def _():
                            out[at] += jnp.dot(
                                a_ref[s, 2 * core + il], b_ref[s], preferred_element_type=jnp.float32
                            )

    return kernel


def contract(kp, flags, a3, pieces):
    w = a3.shape[2]
    inside = pl.BlockSpec(memory_space=pltpu.VMEM)
    out = [jax.ShapeDtypeStruct((4, 2, w, w), jnp.float32)] * 2
    return pl.pallas_call(
        make_contract_kernel(kp),
        in_specs=[pl.BlockSpec(memory_space=pltpu.SMEM)] + [inside] * (len(pieces) + 1),
        out_specs=[inside] * len(out),
        scratch_shapes=[pltpu.VMEM((4, 3 * w, w), jnp.bfloat16)],
        out_shape=out,
        compiler_params=pltpu.CompilerParams(vmem_limit_bytes=28 * MIB),
        cost_estimate=pl.CostEstimate(flops=COST[kp] * 10**9, bytes_accessed=8 * MIB, transcendentals=0),
        name="contract",
    )(flags, a3, *pieces)


def on_device(amp, integ, resid, triples):
    w = amp.shape[-1]
    h = w // 2
    z, c, y, x = (lax.axis_index(n) for n in NAMES)

    tri = triples[0, 0]
    i = tri[0] // 32
    j = tri[0] % 32
    k = tri[1] % 32
    slot = (((j % 2 * 4 + (k // 2) % 4) * 2 + k % 2) * 4 + k // 8) * 2 + i % 2
    place = lax.broadcasted_iota(jnp.int32, (32, w), 1)
    listed = jnp.sum((place == slot[:, None]).astype(jnp.float32), axis=0, keepdims=True)

    mine = lax.dynamic_index_in_dim(integ, c, 0, keepdims=False)
    other = shift(lax.dynamic_index_in_dim(integ, 1 - c, 0, keepdims=False), "c", 1)
    pairs = jnp.where(c == 0, jnp.stack([mine, other]), jnp.stack([other, mine])).reshape(4, 2, w, w)
    own = lax.dynamic_index_in_dim(pairs, x, 0, keepdims=False)
    own, pairs = lax.optimization_barrier((own, pairs))
    own_r, own_l = shift(own, "z", 1), shift(own, "z", -1)

    came = [
        shift(lax.dynamic_index_in_dim(pairs, lax.rem(x + 4 - s, 4), 0, keepdims=False), "x", -s) for s in (1, 2, 3)
    ]
    rest = [jnp.stack([t[kp] for t in came]) for kp in range(2)]
    own_r, own_l, rest[0], rest[1] = lax.optimization_barrier((own_r, own_l, rest[0], rest[1]))

    def with_flags(parity):
        tile = lax.dynamic_index_in_dim(amp, parity, 1, keepdims=False)
        return jnp.concatenate([tile.reshape(2 * w, w), jnp.broadcast_to(listed, (8, w))])

    a_mine, a_other = with_flags(c), shift(with_flags(1 - c), "c", 1)
    a0 = jnp.where(c == 0, jnp.stack([a_mine, a_other]), jnp.stack([a_other, a_mine]))
    a0, rest[0] = lax.optimization_barrier((a0, rest[0]))
    a_r, a_l = shift(a0, "x", -1), shift(a0, "x", 1)
    a_fa, a_fb = shift(a_r[:1], "x", -1), shift(a_l[1:], "x", 1)
    a3 = split_amp(a0, a_r, a_l, a_fa, a_fb)
    rows = jnp.stack([a0[:, 2 * w, :128], a_r[:, 2 * w, :128],
                      jnp.concatenate([a_fa[:, 2 * w, :128], a_fb[:, 2 * w, :128]]), a_l[:, 2 * w, :128]])
    flags = lax.dynamic_index_in_dim(rows.reshape(4, 2, 8, 16), c * 4 + x, 2, keepdims=False)
    flags = jnp.concatenate([flags.reshape(-1).astype(jnp.int32), jnp.stack([z, c])])

    two_r = shift(jnp.concatenate([rest[0], own_r[:, :h].reshape(1, w, w)]), "z", 1)
    two_l = shift(jnp.concatenate([rest[0], own_l[:, h:].reshape(1, w, w)]), "z", -1)
    two_r, two_l, rest[1] = lax.optimization_barrier((two_r, two_l, rest[1]))
    far0 = shift(two_r[:3, :h], "z", 1), shift(two_l[:3, h:], "z", -1)
    rest1_r, rest1_l = shift(rest[1], "z", 1), shift(rest[1], "z", -1)
    a3, rest1_r, rest1_l = lax.optimization_barrier((a3, rest1_r, rest1_l))
    far1 = shift(rest1_r[:, :h], "z", 1), shift(rest1_l[:, h:], "z", -1)

    pieces = own, own_r, own_l
    held, away = contract(0, flags, a3, pieces + (rest[0], two_r, two_l, two_r, two_l) + far0)
    part = held + shift(away, "c", 1)
    part = lax.all_to_all(part, "y", 0, 0, tiled=True)
    gate = part
    even = part[0] + part[1] + part[2] + part[3]
    held, away = contract(1, flags, a3, pieces + (rest[1], rest1_r, rest1_l, two_r, two_l) + far1)
    away, gate = lax.optimization_barrier((away, gate))
    part = lax.all_to_all(held + shift(away, "c", 1), "y", 0, 0, tiled=True)
    return resid + jnp.stack([even, part[0] + part[1] + part[2] + part[3]], axis=1)


def solution(mesh):
    fine = Mesh(mesh.devices.reshape(4, 2, 4, 4), NAMES)
    row, col = ("z", "c"), ("y", "x")
    return jax.shard_map(
        on_device,
        mesh=fine,
        in_specs=(P(row, col), P(col, row), P(row, col), P(row, col)),
        out_specs=P(row, col),
        check_vma=False,
    )
```

```python
import jax
import jax.numpy as jnp
from jax import lax
from jax.experimental import pallas as pl
from jax.experimental.pallas import tpu as pltpu
from jax.sharding import Mesh, PartitionSpec as P

NAMES = ("z", "c", "y", "x")
SIZE = {"z": 4, "c": 2, "y": 4, "x": 4}
MIB = 1024 * 1024
COST = (8, 8)

def shift(t, axis, s):
    n = SIZE[axis]
    return lax.ppermute(t, axis, [(i, (i + s) % n) for i in range(n)])


def halves(a):
    hi = a.astype(jnp.bfloat16)
    return hi, (a - hi.astype(jnp.float32)).astype(jnp.bfloat16)


def split_kernel(a_ref, r_ref, l_ref, fa_ref, fb_ref, o_ref):
    w = a_ref.shape[-1]

    def put(s, ref):
        for il in range(2):
            hi, lo = halves(ref[0, il * w : il * w + w])
            o_ref[s, il, :, :w] = hi
            o_ref[s, il, :, w : 2 * w] = lo
            o_ref[s, il, :, 2 * w :] = hi

    put(0, a_ref)
    put(1, r_ref)
    put(3, l_ref)

    @pl.when(pl.program_id(0) == 0)
    def _():
        put(2, fa_ref)

    @pl.when(pl.program_id(0) == 1)
    def _():
        put(2, fb_ref)


def split_amp(a, r, l, fa, fb):
    rows, w = a.shape[1:]
    each = pl.BlockSpec((1, rows, w), lambda g: (g, 0, 0))
    only = pl.BlockSpec((1, rows, w), lambda g: (0, 0, 0))
    return pl.pallas_call(
        split_kernel,
        grid=(2,),
        in_specs=[each, each, each, only, only],
        out_specs=pl.BlockSpec((4, 2, w, 3 * w), lambda g: (0, g, 0, 0)),
        out_shape=jax.ShapeDtypeStruct((4, 4, w, 3 * w), jnp.bfloat16),
        compiler_params=pltpu.CompilerParams(vmem_limit_bytes=18 * MIB),
        cost_estimate=pl.CostEstimate(flops=0, bytes_accessed=10 * MIB, transcendentals=0),
        name="split_amp",
    )(a, r, l, fa, fb)


def make_contract_kernel(kp):
    def kernel(flag_ref, a_ref, own, own_r, own_l, rest, two_r, two_l, own_fa, own_fb, fa, fb, *refs):
        outs, b_ref = refs[:-1], refs[-1]
        w = b_ref.shape[2]
        h = w // 2

        def load(s, b, at=0):
            n = b.shape[0]
            hi, lo = halves(b)
            b_ref[s, at : at + n] = hi
            b_ref[s, w + at : w + at + n] = hi
            b_ref[s, 2 * w + at : 2 * w + at + n] = lo

        z, c = flag_ref[128], flag_ref[129]

        @pl.loop(0, 4)
        def _(step):
            ka = lax.rem(z + jnp.where(step == 1, 3, jnp.where(step == 2, 1, jnp.where(step == 3, 2, 0))), 4)
            for at, (mine, others) in enumerate(((own, rest), (own_r, two_r), (own_l, two_l))):
                @pl.when(step == at)
                def _():
                    load(0, mine[kp])
                    for s in range(3):
                        load(s + 1, others[s])

            @pl.when(step == 3)
            def _():
                for part, (mine, others) in enumerate(((own_fa, fa), (own_fb, fb))):
                    load(0, mine[3, kp * h : kp * h + h], part * h)
                    for s in range(3):
                        load(s + 1, others[s], part * h)

            for turn in range(2):
                core = lax.rem(c + turn, 2)
                for il in range(2):
                    out, at = outs[turn], (ka, il)
                    out[at] = jnp.zeros((w, w), jnp.float32)
                    for s in range(4):
                        @pl.when(flag_ref[(s * 2 + core) * 16 + kp * 8 + ka * 2 + il] != 0)
                        def _():
                            out[at] += jnp.dot(
                                a_ref[s, 2 * core + il], b_ref[s], preferred_element_type=jnp.float32
                            )

    return kernel


def contract(kp, flags, a3, pieces):
    w = a3.shape[2]
    inside = pl.BlockSpec(memory_space=pltpu.VMEM)
    out = [jax.ShapeDtypeStruct((4, 2, w, w), jnp.float32)] * 2
    return pl.pallas_call(
        make_contract_kernel(kp),
        in_specs=[pl.BlockSpec(memory_space=pltpu.SMEM)] + [inside] * (len(pieces) + 1),
        out_specs=[inside] * len(out),
        scratch_shapes=[pltpu.VMEM((4, 3 * w, w), jnp.bfloat16)],
        out_shape=out,
        compiler_params=pltpu.CompilerParams(vmem_limit_bytes=28 * MIB),
        cost_estimate=pl.CostEstimate(flops=COST[kp] * 10**9, bytes_accessed=8 * MIB, transcendentals=0),
        name="contract",
    )(flags, a3, *pieces)


def on_device(amp, integ, resid, triples):
    w = amp.shape[-1]
    h = w // 2
    z, c, y, x = (lax.axis_index(n) for n in NAMES)

    tri = triples[0, 0]
    i = tri[0] // 32
    j = tri[0] % 32
    k = tri[1] % 32
    slot = (((j % 2 * 4 + (k // 2) % 4) * 2 + k % 2) * 4 + k // 8) * 2 + i % 2
    place = lax.broadcasted_iota(jnp.int32, (32, w), 1)
    listed = jnp.sum((place == slot[:, None]).astype(jnp.float32), axis=0, keepdims=True)

    mine = lax.dynamic_index_in_dim(integ, c, 0, keepdims=False)
    other = shift(lax.dynamic_index_in_dim(integ, 1 - c, 0, keepdims=False), "c", 1)
    pairs = jnp.where(c == 0, jnp.stack([mine, other]), jnp.stack([other, mine])).reshape(4, 2, w, w)
    own = lax.dynamic_index_in_dim(pairs, x, 0, keepdims=False)
    own, pairs = lax.optimization_barrier((own, pairs))
    own_r, own_l = shift(own, "z", 1), shift(own, "z", -1)

    came = [
        shift(lax.dynamic_index_in_dim(pairs, lax.rem(x + 4 - s, 4), 0, keepdims=False), "x", -s) for s in (1, 2, 3)
    ]
    rest = [jnp.stack([t[kp] for t in came]) for kp in range(2)]
    own_r, own_l, rest[0], rest[1] = lax.optimization_barrier((own_r, own_l, rest[0], rest[1]))

    def with_flags(parity):
        tile = lax.dynamic_index_in_dim(amp, parity, 1, keepdims=False)
        return jnp.concatenate([tile.reshape(2 * w, w), jnp.broadcast_to(listed, (8, w))])

    a_mine, a_other = with_flags(c), shift(with_flags(1 - c), "c", 1)
    a0 = jnp.where(c == 0, jnp.stack([a_mine, a_other]), jnp.stack([a_other, a_mine]))
    a0, rest[0] = lax.optimization_barrier((a0, rest[0]))
    a_r, a_l = shift(a0, "x", -1), shift(a0, "x", 1)
    a_fa, a_fb = shift(a_r[:1], "x", -1), shift(a_l[1:], "x", 1)
    a3 = split_amp(a0, a_r, a_l, a_fa, a_fb)
    rows = jnp.stack([a0[:, 2 * w, :128], a_r[:, 2 * w, :128],
                      jnp.concatenate([a_fa[:, 2 * w, :128], a_fb[:, 2 * w, :128]]), a_l[:, 2 * w, :128]])
    flags = lax.dynamic_index_in_dim(rows.reshape(4, 2, 8, 16), c * 4 + x, 2, keepdims=False)
    flags = jnp.concatenate([flags.reshape(-1).astype(jnp.int32), jnp.stack([z, c])])

    two_r = shift(jnp.concatenate([rest[0], own_r[:, :h].reshape(1, w, w)]), "z", 1)
    two_l = shift(jnp.concatenate([rest[0], own_l[:, h:].reshape(1, w, w)]), "z", -1)
    two_r, two_l, rest[1] = lax.optimization_barrier((two_r, two_l, rest[1]))
    far0 = shift(two_r[:3, :h], "z", 1), shift(two_l[:3, h:], "z", -1)
    rest1_r, rest1_l = shift(rest[1], "z", 1), shift(rest[1], "z", -1)
    a3, rest1_r, rest1_l = lax.optimization_barrier((a3, rest1_r, rest1_l))
    far1 = shift(rest1_r[:, :h], "z", 1), shift(rest1_l[:, h:], "z", -1)

    pieces = own, own_r, own_l
    held, away = contract(0, flags, a3, pieces + (rest[0], two_r, two_l, two_r, two_l) + far0)
    part = held + shift(away, "c", 1)
    part = lax.all_to_all(part, "y", 0, 0, tiled=True)
    gate = part
    even = part[0] + part[1] + part[2] + part[3]
    held, away = contract(1, flags, a3, pieces + (rest[1], rest1_r, rest1_l, two_r, two_l) + far1)
    away, gate = lax.optimization_barrier((away, gate))
    part = lax.all_to_all(held + shift(away, "c", 1), "y", 0, 0, tiled=True)
    return resid + jnp.stack([even, part[0] + part[1] + part[2] + part[3]], axis=1)


def solution(mesh):
    fine = Mesh(mesh.devices.reshape(4, 2, 4, 4), NAMES)
    row, col = ("z", "c"), ("y", "x")
    return jax.shard_map(
        on_device,
        mesh=fine,
        in_specs=(P(row, col), P(col, row), P(row, col), P(row, col)),
        out_specs=P(row, col),
        check_vma=False,
    )
```

```python
import jax
import jax.numpy as jnp
from jax import lax
from jax.experimental import pallas as pl
from jax.experimental.pallas import tpu as pltpu
from jax.sharding import Mesh, PartitionSpec as P

NAMES = ("z", "c", "y", "x")
SIZE = {"z": 4, "c": 2, "y": 4, "x": 4}
MIB = 1024 * 1024
COST = (40, 40)

def shift(t, axis, s):
    n = SIZE[axis]
    return lax.ppermute(t, axis, [(i, (i + s) % n) for i in range(n)])


def halves(a):
    hi = a.astype(jnp.bfloat16)
    return hi, (a - hi.astype(jnp.float32)).astype(jnp.bfloat16)


def split_kernel(a_ref, r_ref, l_ref, fa_ref, fb_ref, o_ref):
    w = a_ref.shape[-1]

    def put(s, ref):
        for il in range(2):
            hi, lo = halves(ref[0, il * w : il * w + w])
            o_ref[s, il, :, :w] = hi
            o_ref[s, il, :, w : 2 * w] = lo
            o_ref[s, il, :, 2 * w :] = hi

    put(0, a_ref)
    put(1, r_ref)
    put(3, l_ref)

    @pl.when(pl.program_id(0) == 0)
    def _():
        put(2, fa_ref)

    @pl.when(pl.program_id(0) == 1)
    def _():
        put(2, fb_ref)


def split_amp(a, r, l, fa, fb):
    rows, w = a.shape[1:]
    each = pl.BlockSpec((1, rows, w), lambda g: (g, 0, 0))
    only = pl.BlockSpec((1, rows, w), lambda g: (0, 0, 0))
    return pl.pallas_call(
        split_kernel,
        grid=(2,),
        in_specs=[each, each, each, only, only],
        out_specs=pl.BlockSpec((4, 2, w, 3 * w), lambda g: (0, g, 0, 0)),
        out_shape=jax.ShapeDtypeStruct((4, 4, w, 3 * w), jnp.bfloat16),
        compiler_params=pltpu.CompilerParams(vmem_limit_bytes=18 * MIB),
        cost_estimate=pl.CostEstimate(flops=0, bytes_accessed=10 * MIB, transcendentals=0),
        name="split_amp",
    )(a, r, l, fa, fb)


def make_contract_kernel(kp):
    def kernel(flag_ref, a_ref, own, own_r, own_l, rest, two_r, two_l, own_fa, own_fb, fa, fb, *refs):
        outs, b_ref = refs[:-1], refs[-1]
        w = b_ref.shape[2]
        h = w // 2

        def load(s, b, at=0):
            n = b.shape[0]
            hi, lo = halves(b)
            b_ref[s, at : at + n] = hi
            b_ref[s, w + at : w + at + n] = hi
            b_ref[s, 2 * w + at : 2 * w + at + n] = lo

        z, c = flag_ref[128], flag_ref[129]

        @pl.loop(0, 4)
        def _(step):
            ka = lax.rem(z + jnp.where(step == 1, 3, jnp.where(step == 2, 1, jnp.where(step == 3, 2, 0))), 4)
            for at, (mine, others) in enumerate(((own, rest), (own_r, two_r), (own_l, two_l))):
                @pl.when(step == at)
                def _():
                    load(0, mine[kp])
                    for s in range(3):
                        load(s + 1, others[s])

            @pl.when(step == 3)
            def _():
                for part, (mine, others) in enumerate(((own_fa, fa), (own_fb, fb))):
                    load(0, mine[3, kp * h : kp * h + h], part * h)
                    for s in range(3):
                        load(s + 1, others[s], part * h)

            for turn in range(2):
                core = lax.rem(c + turn, 2)
                for il in range(2):
                    out, at = outs[turn], (ka, il)
                    out[at] = jnp.zeros((w, w), jnp.float32)
                    for s in range(4):
                        @pl.when(flag_ref[(s * 2 + core) * 16 + kp * 8 + ka * 2 + il] != 0)
                        def _():
                            out[at] += jnp.dot(
                                a_ref[s, 2 * core + il], b_ref[s], preferred_element_type=jnp.float32
                            )

    return kernel


def contract(kp, flags, a3, pieces):
    w = a3.shape[2]
    inside = pl.BlockSpec(memory_space=pltpu.VMEM)
    out = [jax.ShapeDtypeStruct((4, 2, w, w), jnp.float32)] * 2
    return pl.pallas_call(
        make_contract_kernel(kp),
        in_specs=[pl.BlockSpec(memory_space=pltpu.SMEM)] + [inside] * (len(pieces) + 1),
        out_specs=[inside] * len(out),
        scratch_shapes=[pltpu.VMEM((4, 3 * w, w), jnp.bfloat16)],
        out_shape=out,
        compiler_params=pltpu.CompilerParams(vmem_limit_bytes=28 * MIB),
        cost_estimate=pl.CostEstimate(flops=COST[kp] * 10**9, bytes_accessed=8 * MIB, transcendentals=0),
        name="contract",
    )(flags, a3, *pieces)


def on_device(amp, integ, resid, triples):
    w = amp.shape[-1]
    h = w // 2
    z, c, y, x = (lax.axis_index(n) for n in NAMES)

    tri = triples[0, 0]
    i = tri[0] // 32
    j = tri[0] % 32
    k = tri[1] % 32
    slot = (((j % 2 * 4 + (k // 2) % 4) * 2 + k % 2) * 4 + k // 8) * 2 + i % 2
    place = lax.broadcasted_iota(jnp.int32, (32, w), 1)
    listed = jnp.sum((place == slot[:, None]).astype(jnp.float32), axis=0, keepdims=True)

    mine = lax.dynamic_index_in_dim(integ, c, 0, keepdims=False)
    other = shift(lax.dynamic_index_in_dim(integ, 1 - c, 0, keepdims=False), "c", 1)
    pairs = jnp.where(c == 0, jnp.stack([mine, other]), jnp.stack([other, mine])).reshape(4, 2, w, w)
    own = lax.dynamic_index_in_dim(pairs, x, 0, keepdims=False)
    own, pairs = lax.optimization_barrier((own, pairs))
    own_r, own_l = shift(own, "z", 1), shift(own, "z", -1)

    came = [
        shift(lax.dynamic_index_in_dim(pairs, lax.rem(x + 4 - s, 4), 0, keepdims=False), "x", -s) for s in (1, 2, 3)
    ]
    rest = [jnp.stack([t[kp] for t in came]) for kp in range(2)]
    own_r, own_l, rest[0], rest[1] = lax.optimization_barrier((own_r, own_l, rest[0], rest[1]))

    def with_flags(parity):
        tile = lax.dynamic_index_in_dim(amp, parity, 1, keepdims=False)
        return jnp.concatenate([tile.reshape(2 * w, w), jnp.broadcast_to(listed, (8, w))])

    a_mine, a_other = with_flags(c), shift(with_flags(1 - c), "c", 1)
    a0 = jnp.where(c == 0, jnp.stack([a_mine, a_other]), jnp.stack([a_other, a_mine]))
    a0, rest[0] = lax.optimization_barrier((a0, rest[0]))
    a_r, a_l = shift(a0, "x", -1), shift(a0, "x", 1)
    a_fa, a_fb = shift(a_r[:1], "x", -1), shift(a_l[1:], "x", 1)
    a3 = split_amp(a0, a_r, a_l, a_fa, a_fb)
    rows = jnp.stack([a0[:, 2 * w, :128], a_r[:, 2 * w, :128],
                      jnp.concatenate([a_fa[:, 2 * w, :128], a_fb[:, 2 * w, :128]]), a_l[:, 2 * w, :128]])
    flags = lax.dynamic_index_in_dim(rows.reshape(4, 2, 8, 16), c * 4 + x, 2, keepdims=False)
    flags = jnp.concatenate([flags.reshape(-1).astype(jnp.int32), jnp.stack([z, c])])

    two_r = shift(jnp.concatenate([rest[0], own_r[:, :h].reshape(1, w, w)]), "z", 1)
    two_l = shift(jnp.concatenate([rest[0], own_l[:, h:].reshape(1, w, w)]), "z", -1)
    two_r, two_l, rest[1] = lax.optimization_barrier((two_r, two_l, rest[1]))
    far0 = shift(two_r[:3, :h], "z", 1), shift(two_l[:3, h:], "z", -1)
    rest1_r, rest1_l = shift(rest[1], "z", 1), shift(rest[1], "z", -1)
    a3, rest1_r, rest1_l = lax.optimization_barrier((a3, rest1_r, rest1_l))
    far1 = shift(rest1_r[:, :h], "z", 1), shift(rest1_l[:, h:], "z", -1)

    pieces = own, own_r, own_l
    held, away = contract(0, flags, a3, pieces + (rest[0], two_r, two_l, two_r, two_l) + far0)
    part = held + shift(away, "c", 1)
    part = lax.all_to_all(part, "y", 0, 0, tiled=True)
    gate = part
    even = part[0] + part[1] + part[2] + part[3]
    held, away = contract(1, flags, a3, pieces + (rest[1], rest1_r, rest1_l, two_r, two_l) + far1)
    last, gate = lax.optimization_barrier((away[:, 1:], gate))
    away = jnp.concatenate([shift(away[:, :1], "c", 1), shift(last, "c", 1)], axis=1)
    part = lax.all_to_all(held + away, "y", 0, 0, tiled=True)
    return resid + jnp.stack([even, part[0] + part[1] + part[2] + part[3]], axis=1)


def solution(mesh):
    fine = Mesh(mesh.devices.reshape(4, 2, 4, 4), NAMES)
    row, col = ("z", "c"), ("y", "x")
    return jax.shard_map(
        on_device,
        mesh=fine,
        in_specs=(P(row, col), P(col, row), P(row, col), P(row, col)),
        out_specs=P(row, col),
        check_vma=False,
    )
```
